32 devices in a mesh: dp: 8 (over y, x, core), tensor: 4 (over z).
Axes of the slice: x: 2, y: 2, z: 4, core: 2. Of those that a mesh axis runs over, the one named last changes fastest.
Arguments:
- text: bfloat16 [8192, 768], P(('dp', 'tensor')), may hold values from -6 to 6
- image: bfloat16 [2304, 1024], P(('dp', 'tensor')), may hold values from -6 to 6
- text_segment: int32 [64, 128], P('dp'), may hold values from 0 to 3, as said below
- image_segment: int32 [64, 36], P('dp'), may hold values from 0 to 3, as said below
- text_cross_weight: bfloat16 [768, 3, 1024], P(None, None, 'tensor'), may hold values from -0.21875 to 0.21875
- text_cross_bias: bfloat16 [2, 1024], P(None, 'tensor'), may hold values from -3 to 3
- text_cross_output: bfloat16 [1024, 768], P('tensor'), may hold values from -0.5 to 0.5
- text_inner_expand: bfloat16 [768, 3072], P(None, 'tensor'), may hold values from -0.21875 to 0.21875
- text_inner_offset: bfloat16 [3072], P('tensor'), may hold values from -3 to 3
- text_inner_reduce: bfloat16 [3072, 768], P('tensor'), may hold values from -0.15625 to 0.15625
- text_self_weight: bfloat16 [768, 3, 768], P(None, None, 'tensor'), may hold values from -0.21875 to 0.21875
- text_self_bias: bfloat16 [2, 768], P(None, 'tensor'), may hold values from -3 to 3
- text_self_output: bfloat16 [768, 768], P('tensor'), may hold values from -1.25 to 1.25
- text_outer_expand: bfloat16 [768, 3072], P(None, 'tensor'), may hold values from -0.21875 to 0.21875
- text_outer_offset: bfloat16 [3072], P('tensor'), may hold values from -3 to 3
- text_outer_reduce: bfloat16 [3072, 768], P('tensor'), may hold values from -0.15625 to 0.15625
- text_branch_bias: bfloat16 [4, 768], replicated, may hold values from -2 to 2
- text_norm_gain: bfloat16 [4, 768], replicated, may hold values from 0.099609375 to 1.8984375
- text_norm_shift: bfloat16 [4, 768], replicated, may hold values from -2 to 2
- image_cross_weight: bfloat16 [1024, 3, 1024], P(None, None, 'tensor'), may hold values from -0.1875 to 0.1875
- image_cross_bias: bfloat16 [2, 1024], P(None, 'tensor'), may hold values from -3 to 3
- image_cross_output: bfloat16 [1024, 1024], P('tensor'), may hold values from -1 to 1
- image_inner_expand: bfloat16 [1024, 1024], P(None, 'tensor'), may hold values from -0.1875 to 0.1875
- image_inner_offset: bfloat16 [1024], P('tensor'), may hold values from -3 to 3
- image_inner_reduce: bfloat16 [1024, 1024], P('tensor'), may hold values from -0.25 to 0.25
- image_self_weight: bfloat16 [1024, 3, 1024], P(None, None, 'tensor'), may hold values from -0.1875 to 0.1875
- image_self_bias: bfloat16 [2, 1024], P(None, 'tensor'), may hold values from -3 to 3
- image_self_output: bfloat16 [1024, 1024], P('tensor'), may hold values from -0.5 to 0.5
- image_outer_expand: bfloat16 [1024, 1024], P(None, 'tensor'), may hold values from -0.1875 to 0.1875
- image_outer_offset: bfloat16 [1024], P('tensor'), may hold values from -3 to 3
- image_outer_reduce: bfloat16 [1024, 1024], P('tensor'), may hold values from -0.25 to 0.25
- image_branch_bias: bfloat16 [4, 1024], replicated, may hold values from -2 to 2
- image_norm_gain: bfloat16 [4, 1024], replicated, may hold values from 0.099609375 to 1.8984375
- image_norm_shift: bfloat16 [4, 1024], replicated, may hold values from -2 to 2
- text_cotangent: bfloat16 [8192, 768], P(('dp', 'tensor')), may hold values from -6 to 6
- image_cotangent: bfloat16 [2304, 1024], P(('dp', 'tensor')), may hold values from -6 to 6
Outputs:
- text_result: float32 [8192, 768], P(('dp', 'tensor'))
- image_result: float32 [2304, 1024], P(('dp', 'tensor'))
- delta_text: float32 [8192, 768], P(('dp', 'tensor'))
- delta_image: float32 [2304, 1024], P(('dp', 'tensor'))
- delta_text_cross_weight: float32 [768, 3, 1024], P('dp', None, 'tensor')
- delta_text_cross_bias: float32 [2, 1024], P(None, 'tensor')
- delta_text_cross_output: float32 [1024, 768], P('tensor', 'dp')
- delta_text_inner_expand: float32 [768, 3072], P('dp', 'tensor')
- delta_text_inner_offset: float32 [3072], P('tensor')
- delta_text_inner_reduce: float32 [3072, 768], P('tensor', 'dp')
- delta_text_self_weight: float32 [768, 3, 768], P('dp', None, 'tensor')
- delta_text_self_bias: float32 [2, 768], P(None, 'tensor')
- delta_text_self_output: float32 [768, 768], P('tensor', 'dp')
- delta_text_outer_expand: float32 [768, 3072], P('dp', 'tensor')
- delta_text_outer_offset: float32 [3072], P('tensor')
- delta_text_outer_reduce: float32 [3072, 768], P('tensor', 'dp')
- delta_text_branch_bias: float32 [4, 768], replicated
- delta_text_norm_gain: float32 [4, 768], replicated
- delta_text_norm_shift: float32 [4, 768], replicated
- delta_image_cross_weight: float32 [1024, 3, 1024], P('dp', None, 'tensor')
- delta_image_cross_bias: float32 [2, 1024], P(None, 'tensor')
- delta_image_cross_output: float32 [1024, 1024], P('tensor', 'dp')
- delta_image_inner_expand: float32 [1024, 1024], P('dp', 'tensor')
- delta_image_inner_offset: float32 [1024], P('tensor')
- delta_image_inner_reduce: float32 [1024, 1024], P('tensor', 'dp')
- delta_image_self_weight: float32 [1024, 3, 1024], P('dp', None, 'tensor')
- delta_image_self_bias: float32 [2, 1024], P(None, 'tensor')
- delta_image_self_output: float32 [1024, 1024], P('tensor', 'dp')
- delta_image_outer_expand: float32 [1024, 1024], P('dp', 'tensor')
- delta_image_outer_offset: float32 [1024], P('tensor')
- delta_image_outer_reduce: float32 [1024, 1024], P('tensor', 'dp')
- delta_image_branch_bias: float32 [4, 1024], replicated
- delta_image_norm_gain: float32 [4, 1024], replicated
- delta_image_norm_shift: float32 [4, 1024], replicated
The draws below stay inside these ranges and needn't reach their ends.
Inputs may be any that keep to these rules, and one draw needn't show every extreme that they name: `text_segment`: along each row the caption numbers never fall and every number 0 to 3 appears in every row. `image_segment`: along each row the image numbers never fall and every number 0 to 3 appears in every row.
All inputs are finite; a program needn't handle non-finite values.
Results may differ from the reference program's by a relative error of at most 0.035.
Values may be sent and summed in bfloat16 or wider, within the bound.
A program may use at most 192 MiB of HBM per device.

```python
import math
import jax
import jax.numpy as jnp
from jax import lax

DT = 768
DV = 1024
CO_DH = 128
TS_DH = 64
VS_DH = 128
HT = 3072
HV = 1024
TOK_ROW = 128
REG_ROW = 36
CAPTIONS = 4
ROW_DEV = 8
ROWS = 64
TEXT_TOKENS = 8192
REGIONS = 2304
CO_WIDTH = 1024
TS_WIDTH = 768
VS_WIDTH = 1024
N_DP = 8


def segment_rows(key, length):
    half = length // (2 * CAPTIONS)
    jitter = jax.random.randint(key, (ROWS, CAPTIONS - 1), 1 - half, half)
    cuts = jnp.arange(1, CAPTIONS, dtype=jnp.int32)[None, :] * (length // CAPTIONS) + jitter
    places = jnp.arange(length, dtype=jnp.int32)
    return jnp.sum((places[None, :, None] >= cuts[:, None, :]).astype(jnp.int32), axis=2).astype(jnp.int32)


def draw_text_segment(key, part):
    return segment_rows(jax.random.fold_in(key, 11), TOK_ROW)


def draw_image_segment(key, part):
    return segment_rows(jax.random.fold_in(key, 23), REG_ROW)


def with_spikes(array, stream_key, source, target, shards_of, factor):
    def block_of(axis_at):
        return (jnp.arange(array.shape[axis_at]) // (array.shape[axis_at] // shards_of)).reshape((-1,) + (1,) * (array.ndim - 1 - axis_at))

    one_side = jax.random.permutation(stream_key, shards_of)[block_of(target)]
    other_side = (block_of(target) + shards_of // 2) % shards_of
    return jnp.where((block_of(source) == one_side) | (block_of(source) == other_side), factor * array, array)


def level_of(rng, dims, cuts, low, top_value):
    def one(dim, shards_of):
        steps = jax.random.uniform(jax.random.fold_in(jax.random.fold_in(rng, 6), dim), (shards_of,), jnp.float32, low / len(cuts), top_value / len(cuts))
        return jnp.repeat(jnp.exp(steps), dims[dim] // shards_of).reshape((-1,) + (1,) * (len(dims) - dim - 1))

    factor_of = one(*cuts[0])
    for cut in cuts[1:]:
        factor_of = factor_of * one(*cut)
    return factor_of


def centred(own_key, dims, width, limit, shards=(), kind=jnp.bfloat16):
    level = level_of(own_key, dims, shards, -0.22, 0.18) if shards else 1.0
    drawn = jax.random.normal(own_key, dims, jnp.float32) * width * level
    return jnp.minimum(jnp.maximum(drawn, -limit), limit).astype(kind)


def gaussian_with(own_key, shape, scale, most, cuts, heavy, kind=jnp.bfloat16):
    result = scale * jax.random.normal(own_key, shape, jnp.float32)
    if cuts:
        result = result * level_of(own_key, shape, cuts, -0.22, 0.18)
    return jnp.clip(with_spikes(result, jax.random.fold_in(own_key, 3), *heavy), -most, most).astype(kind)


def setup_inputs(seed: int = 0) -> dict:
    key_list = jax.random.split(jax.random.key(seed), 37)
    return {
        "text": gaussian_with(key_list[0], (TEXT_TOKENS, DT), 1.0, 6.0, ((0, 32),), (0, 1, 32, 2.75)),
        "image": gaussian_with(key_list[1], (REGIONS, DV), 1.0, 6.0, ((0, 32),), (0, 1, 32, 2.75)),
        "text_segment": draw_text_segment(jax.random.fold_in(key_list[36], 71), 0),
        "image_segment": draw_image_segment(jax.random.fold_in(key_list[36], 71), 0),
        "text_cross_weight": centred(key_list[4], (DT, 3, CO_WIDTH), DT ** -0.5, 0.21875, ((2, 4),)),
        "text_cross_bias": centred(key_list[5], (2, CO_WIDTH), 0.5, 3.0, ((1, 4),)),
        "text_cross_output": centred(key_list[6], (CO_WIDTH, DT), (CO_WIDTH * CAPTIONS // REG_ROW) ** -0.5, 0.5, ((0, 4),)),
        "text_inner_expand": centred(key_list[7], (DT, HT), DT ** -0.5, 0.21875, ((1, 4),)),
        "text_inner_offset": centred(key_list[8], (HT,), 0.5, 3.0, ((0, 4),)),
        "text_inner_reduce": centred(key_list[9], (HT, DT), (HT // 2) ** -0.5, 0.15625, ((0, 4),)),
        "text_self_weight": centred(key_list[10], (DT, 3, TS_WIDTH), DT ** -0.5, 0.21875, ((2, 4),)),
        "text_self_bias": centred(key_list[11], (2, TS_WIDTH), 0.5, 3.0, ((1, 4),)),
        "text_self_output": centred(key_list[12], (TS_WIDTH, DT), (TS_WIDTH * CAPTIONS // TOK_ROW) ** -0.5, 1.25, ((0, 4),)),
        "text_outer_expand": centred(key_list[13], (DT, HT), DT ** -0.5, 0.21875, ((1, 4),)),
        "text_outer_offset": centred(key_list[14], (HT,), 0.5, 3.0, ((0, 4),)),
        "text_outer_reduce": centred(key_list[15], (HT, DT), (HT // 2) ** -0.5, 0.15625, ((0, 4),)),
        "text_branch_bias": centred(key_list[16], (4, DT), 0.3, 2.0),
        "text_norm_gain": jnp.clip(1.0 + 0.18 * jax.random.normal(key_list[17], (4, DT), jnp.float32), 0.099609375, 1.8984375).astype(jnp.bfloat16),
        "text_norm_shift": centred(key_list[18], (4, DT), 0.3, 2.0),
        "image_cross_weight": centred(key_list[19], (DV, 3, CO_WIDTH), DV ** -0.5, 0.1875, ((2, 4),)),
        "image_cross_bias": centred(key_list[20], (2, CO_WIDTH), 0.5, 3.0, ((1, 4),)),
        "image_cross_output": centred(key_list[21], (CO_WIDTH, DV), (CO_WIDTH * CAPTIONS // TOK_ROW) ** -0.5, 1.0, ((0, 4),)),
        "image_inner_expand": centred(key_list[22], (DV, HV), DV ** -0.5, 0.1875, ((1, 4),)),
        "image_inner_offset": centred(key_list[23], (HV,), 0.5, 3.0, ((0, 4),)),
        "image_inner_reduce": centred(key_list[24], (HV, DV), (HV // 2) ** -0.5, 0.25, ((0, 4),)),
        "image_self_weight": centred(key_list[25], (DV, 3, VS_WIDTH), DV ** -0.5, 0.1875, ((2, 4),)),
        "image_self_bias": centred(key_list[26], (2, VS_WIDTH), 0.5, 3.0, ((1, 4),)),
        "image_self_output": centred(key_list[27], (VS_WIDTH, DV), (VS_WIDTH * CAPTIONS // REG_ROW) ** -0.5, 0.5, ((0, 4),)),
        "image_outer_expand": centred(key_list[28], (DV, HV), DV ** -0.5, 0.1875, ((1, 4),)),
        "image_outer_offset": centred(key_list[29], (HV,), 0.5, 3.0, ((0, 4),)),
        "image_outer_reduce": centred(key_list[30], (HV, DV), (HV // 2) ** -0.5, 0.25, ((0, 4),)),
        "image_branch_bias": centred(key_list[31], (4, DV), 0.3, 2.0),
        "image_norm_gain": jnp.clip(1.0 + 0.18 * jax.random.normal(key_list[32], (4, DV), jnp.float32), 0.099609375, 1.8984375).astype(jnp.bfloat16),
        "image_norm_shift": centred(key_list[33], (4, DV), 0.3, 2.0),
        "text_cotangent": gaussian_with(key_list[34], (TEXT_TOKENS, DT), 1.0, 6.0, ((0, 32),), (0, 1, 32, 2.75)),
        "image_cotangent": gaussian_with(key_list[35], (REGIONS, DV), 1.0, 6.0, ((0, 32),), (0, 1, 32, 2.75)),
    }


@jax.custom_vjp
def low(v):
    return lax.optimization_barrier(v.astype(jnp.bfloat16)).astype(jnp.float32)

@jax.custom_vjp
def low_back(v):
    return v

def low_keep(v):
    return (low(v), None)

def low_pass(kept, grad):
    return (grad,)

def back_keep(v):
    return (v, None)

def back_low(kept, grad):
    return (low(grad),)
low.defvjp(low_keep, low_pass)
low_back.defvjp(back_keep, back_low)
norm_eps = 1e-05
root_half = 0.7071067811865476
highest = lax.Precision.HIGHEST

def project(values, weight):
    return jnp.tensordot(values, weight, axes=1, precision=highest)

def normalize(hidden, gain, shift):
    center = hidden - lax.optimization_barrier(jnp.mean(hidden, axis=1, keepdims=True))
    scale = lax.rsqrt(lax.optimization_barrier(jnp.mean(center * center, axis=1, keepdims=True)) + norm_eps)
    return center * scale * gain + shift

def gelu_value(hidden):
    return 0.5 * hidden * (1.0 + jax.scipy.special.erf(hidden * root_half))

def heads_of(values, count, size):
    return values.reshape(count, values.shape[0] // count, -1, size)

def attend(query, key, value, allowed, size):
    scores = jnp.einsum('rqhd,rkhd->rhqk', query, key, precision=highest) * (1.0 / math.sqrt(size))
    scores = low_back(jnp.where(allowed[:, None], scores, -1e+30))
    probs = low(jax.nn.softmax(scores, axis=3))
    context = jnp.einsum('rhqk,rkhd->rqhd', probs, value, precision=highest)
    context = context.reshape(context.shape[0] * context.shape[1], -1)
    return low(low_back(context))

def project_heads(values, weight, bias):
    mixed = project(values, weight)
    offset = jnp.stack([bias[0], jnp.zeros_like(bias[0]), bias[1]])
    return low(low_back(mixed + offset[None]))

def feed(state, expand, offset, reduce_weight, bias, gain, shift):
    hidden = low_back(project(low(state), expand) + offset)
    active = low(gelu_value(hidden))
    return normalize(state + low_back(project(active, reduce_weight) + bias), gain, shift)

def self_block(state, weight, bias, output, row_bias, gain, shift, allowed, count, size):
    mixed = project_heads(low(state), weight, bias)
    context = attend(heads_of(mixed[:, 0], count, size), heads_of(mixed[:, 1], count, size), heads_of(mixed[:, 2], count, size), allowed, size)
    return normalize(state + low_back(project(context, output) + row_bias), gain, shift)

def layer(weights, text, image, text_segment, image_segment):
    text_cross_weight, text_cross_bias, text_cross_output, text_inner_expand, text_inner_offset, text_inner_reduce, text_self_weight, text_self_bias, text_self_output, text_outer_expand, text_outer_offset, text_outer_reduce, text_branch_bias, text_norm_gain, text_norm_shift, image_cross_weight, image_cross_bias, image_cross_output, image_inner_expand, image_inner_offset, image_inner_reduce, image_self_weight, image_self_bias, image_self_output, image_outer_expand, image_outer_offset, image_outer_reduce, image_branch_bias, image_norm_gain, image_norm_shift = weights
    count = text_segment.shape[0]
    cross_text = text_segment[:, :, None] == image_segment[:, None, :]
    cross_image = jnp.transpose(cross_text, (0, 2, 1))
    self_text = text_segment[:, :, None] == text_segment[:, None, :]
    self_image = image_segment[:, :, None] == image_segment[:, None, :]
    text_mixed = project_heads(text, text_cross_weight, text_cross_bias)
    image_mixed = project_heads(image, image_cross_weight, image_cross_bias)
    text_context = attend(heads_of(text_mixed[:, 0], count, CO_DH), heads_of(image_mixed[:, 1], count, CO_DH), heads_of(image_mixed[:, 2], count, CO_DH), cross_text, CO_DH)
    image_context = attend(heads_of(image_mixed[:, 0], count, CO_DH), heads_of(text_mixed[:, 1], count, CO_DH), heads_of(text_mixed[:, 2], count, CO_DH), cross_image, CO_DH)
    text_state = normalize(text + low_back(project(text_context, text_cross_output) + text_branch_bias[0]), text_norm_gain[0], text_norm_shift[0])
    image_state = normalize(image + low_back(project(image_context, image_cross_output) + image_branch_bias[0]), image_norm_gain[0], image_norm_shift[0])
    text_state = feed(text_state, text_inner_expand, text_inner_offset, text_inner_reduce, text_branch_bias[1], text_norm_gain[1], text_norm_shift[1])
    image_state = feed(image_state, image_inner_expand, image_inner_offset, image_inner_reduce, image_branch_bias[1], image_norm_gain[1], image_norm_shift[1])
    text_state = self_block(text_state, text_self_weight, text_self_bias, text_self_output, text_branch_bias[2], text_norm_gain[2], text_norm_shift[2], self_text, count, TS_DH)
    image_state = self_block(image_state, image_self_weight, image_self_bias, image_self_output, image_branch_bias[2], image_norm_gain[2], image_norm_shift[2], self_image, count, VS_DH)
    text_state = feed(text_state, text_outer_expand, text_outer_offset, text_outer_reduce, text_branch_bias[3], text_norm_gain[3], text_norm_shift[3])
    image_state = feed(image_state, image_outer_expand, image_outer_offset, image_outer_reduce, image_branch_bias[3], image_norm_gain[3], image_norm_shift[3])
    return (text_state, image_state)

def add_pair(first, second):
    return first + second

def reference(text, image, text_segment, image_segment, text_cross_weight, text_cross_bias, text_cross_output, text_inner_expand, text_inner_offset, text_inner_reduce, text_self_weight, text_self_bias, text_self_output, text_outer_expand, text_outer_offset, text_outer_reduce, text_branch_bias, text_norm_gain, text_norm_shift, image_cross_weight, image_cross_bias, image_cross_output, image_inner_expand, image_inner_offset, image_inner_reduce, image_self_weight, image_self_bias, image_self_output, image_outer_expand, image_outer_offset, image_outer_reduce, image_branch_bias, image_norm_gain, image_norm_shift, text_cotangent, image_cotangent):
    weights = tuple((item.astype(jnp.float32) for item in (text_cross_weight, text_cross_bias, text_cross_output, text_inner_expand, text_inner_offset, text_inner_reduce, text_self_weight, text_self_bias, text_self_output, text_outer_expand, text_outer_offset, text_outer_reduce, text_branch_bias, text_norm_gain, text_norm_shift, image_cross_weight, image_cross_bias, image_cross_output, image_inner_expand, image_inner_offset, image_inner_reduce, image_self_weight, image_self_bias, image_self_output, image_outer_expand, image_outer_offset, image_outer_reduce, image_branch_bias, image_norm_gain, image_norm_shift)))
    text_blocks = text.astype(jnp.float32).reshape(N_DP, ROW_DEV * TOK_ROW, DT)
    image_blocks = image.astype(jnp.float32).reshape(N_DP, ROW_DEV * REG_ROW, DV)
    text_marks = text_segment.reshape(N_DP, ROW_DEV, TOK_ROW)
    image_marks = image_segment.reshape(N_DP, ROW_DEV, REG_ROW)
    text_seeds = text_cotangent.astype(jnp.float32).reshape(N_DP, ROW_DEV * TOK_ROW, DT)
    image_seeds = image_cotangent.astype(jnp.float32).reshape(N_DP, ROW_DEV * REG_ROW, DV)

    def block_step(totals, block):
        text_piece, image_piece, text_mark, image_mark, text_seed, image_seed = block

        def forward_pass(params, text_input, image_input):
            return layer(params, text_input, image_input, text_mark, image_mark)
        outputs, backward = jax.vjp(forward_pass, weights, text_piece, image_piece)
        changes = backward((text_seed, image_seed))
        totals = jax.tree.map(add_pair, totals, changes[0])
        return (totals, (outputs[0], outputs[1], changes[1], changes[2]))
    start = jax.tree.map(jnp.zeros_like, weights)
    totals, pieces = lax.scan(block_step, start, (text_blocks, image_blocks, text_marks, image_marks, text_seeds, image_seeds))
    text_result = pieces[0].reshape(TEXT_TOKENS, DT)
    image_result = pieces[1].reshape(REGIONS, DV)
    delta_text = pieces[2].reshape(TEXT_TOKENS, DT)
    delta_image = pieces[3].reshape(REGIONS, DV)
    return (text_result, image_result, delta_text, delta_image, totals[0], totals[1], totals[2], totals[3], totals[4], totals[5], totals[6], totals[7], totals[8], totals[9], totals[10], totals[11], totals[12], totals[13], totals[14], totals[15], totals[16], totals[17], totals[18], totals[19], totals[20], totals[21], totals[22], totals[23], totals[24], totals[25], totals[26], totals[27], totals[28], totals[29])
```

```python
import functools
import math

import jax
import jax.numpy as jnp
from jax import lax
from jax.experimental import pallas as pl
from jax.experimental.pallas import tpu as pltpu
from jax.sharding import PartitionSpec as P

CO_DH = 128
TS_DH = 64
VS_DH = 128
LANES = 256
MESH = pl.DeviceIdType.MESH

norm_eps = 1e-05
root_half = 0.7071067811865476
inv_root_tau = 0.3989422804014327
f32 = jnp.float32
bf16 = jnp.bfloat16


def gelu_value(hidden):
    return 0.5 * hidden * (1.0 + lax.erf(hidden * root_half))


def gelu_slope(hidden):
    return (
        0.5 * (1.0 + lax.erf(hidden * root_half))
        + hidden * jnp.exp(-0.5 * hidden * hidden) * inv_root_tau
    )


def norm_forward(hidden, gain, shift):
    center = hidden - jnp.mean(hidden, axis=1, keepdims=True)
    scale = lax.rsqrt(jnp.mean(center * center, axis=1, keepdims=True) + norm_eps)
    normed = center * scale
    return normed * gain + shift, normed, scale


def norm_backward(upstream, normed, scale, gain):
    inner = upstream * gain
    return scale * (
        inner
        - jnp.mean(inner, axis=1, keepdims=True)
        - normed * jnp.mean(inner * normed, axis=1, keepdims=True)
    )


def times(left, right):
    return jnp.dot(left, right, preferred_element_type=f32)


def times_transpose(left, right):
    return lax.dot_general(left, right, (((1,), (1,)), ((), ())), preferred_element_type=f32)


def outer_sum(left, right):
    return lax.dot_general(left, right, (((0,), (0,)), ((), ())), preferred_element_type=f32)


def swap(value, axis, mask):
    return lax.ppermute(value, axis, [(i, i ^ mask) for i in range(lax.axis_size(axis))])


def segments_of(mats):
    dp, found = lax.axis_size("dp"), []
    for index, (_, parts) in enumerate(mats):
        base = 0
        for total in parts:
            found.append((index, base, total // dp))
            base += total
    return found


def greet(partners):
    barrier = pltpu.get_barrier_semaphore()
    for partner in partners:
        pl.semaphore_signal(barrier, inc=1, device_id=partner, device_id_type=MESH)
    pl.semaphore_wait(barrier, len(partners))


EARLY = (((0, 1), (2, 3)), ((4, 5), (6, 7)), ((8, 8), (9, 10)))
FIRST_TASK = (6, 10, 14)


def early_columns(text_width, image_width, text_hidden, image_hidden, text_own, image_own):
    counts = [text_width, image_width, text_hidden, image_hidden, text_own, image_own]
    counts += [text_hidden, image_hidden]
    found, at = [], 0
    for count in counts:
        found.append((at, count))
        at += count
    return found


def early_outs(jobs, widths, states):
    outs = []
    for stage in range(3):
        for k, state in enumerate(states):
            tokens, width = state.shape
            if stage == 1:
                shapes = [((tokens, 4 * widths[2 + k]), f32), ((tokens, 4 * widths[2 + k]), bf16)]
            else:
                _, _, size, heads, shift = jobs[stage // 2][k]
                columns = (shift or 3 * size * heads) + (size * heads if shift else 0)
                shapes = [((tokens, 4 * columns), bf16), ((tokens, 4 * (shift + size * heads)), bf16)]
            shapes += [((tokens, width), f32), ((tokens, width), f32), ((tokens, 128), f32)]
            outs += shapes
    return outs


def gather_kernel(segments, stage_of, n_mats, jobs, places, shapes, *refs):
    n_in = n_mats + 1
    locals_, refs = refs[:n_in], refs[n_in:]
    states, rows, ids, refs = refs[:2], refs[2:8], refs[8:12], refs[12:]
    outs, refs = refs[:n_in], refs[n_in:]
    results, refs = refs[: len(shapes)], refs[len(shapes) :]
    values, refs = refs[: len(shapes)], refs[len(shapes) :]
    blocks, bias, (send_sems, recv_sems, local_sems) = refs[:4], refs[4], refs[5:]
    me, place_t = lax.axis_index("dp"), lax.axis_index("tensor")
    lines = [{"tensor": jnp.bitwise_xor(place_t, s)} for s in range(1, 4)]
    core, across, along = [{"dp": jnp.bitwise_xor(me, mask)} for mask in (1, 2, 4)]
    greet(lines + [core, across, along])
    copies, moves = [], []

    def copy(source, target, device):
        k = len(copies)
        item = pltpu.make_async_remote_copy(
            source, target, send_sems.at[k], recv_sems.at[k], device_id=device, device_id_type=MESH
        )
        item.start()
        copies.append(item)
        return item

    def move(source, target):
        item = pltpu.make_async_copy(source, target, local_sems.at[len(moves)])
        item.start()
        moves.append(item)
        return item

    def rows_of(segment, mask):
        _, base, count = segment
        return pl.ds(pl.multiple_of(base + jnp.bitwise_xor(me, mask) * count, 8), count)

    def pass_on(segment, mask, device, low=0, high=1):
        index = segment[0]
        width = outs[index].shape[2] // 2
        part = outs[index].at[
            pl.ds(1, 3), rows_of(segment, mask), pl.ds(low * width, (high + 1 - low) * width)
        ]
        return copy(part, part, device)

    late = [[] for _ in range(4)]
    bias_copies = [copy(locals_[-1], outs[-1].at[s], lines[s]) for s in range(3)]
    arrivals = []
    for segment in segments:
        index, part = segment[0], rows_of(segment, 0)
        arrivals.append(
            [copy(locals_[index].at[part], outs[index].at[s + 1, part], lines[s]) for s in range(3)]
        )
    for index in range(n_mats):
        late[stage_of[index]].append(copy(locals_[index], outs[index].at[0], core))

    loads, finished = {}, []
    values_of = [
        [values[(2 * stage + k) * 5 : (2 * stage + k + 1) * 5] for k in range(2)] for stage in range(3)
    ]

    def load(stage, s):
        slot, items = s % 2, []
        for k in range(2):
            for part in range(2):
                if part and EARLY[stage][k][0] == EARLY[stage][k][1]:
                    continue
                source = outs[EARLY[stage][k][part]]
                items.append(
                    move(source.at[s], blocks[2 * k + part].at[slot, pl.ds(0, source.shape[1])])
                )
        loads[stage, s] = items

    def run(stage, s):
        if s == 0:
            for item in late[stage]:
                item.wait_recv()
            if stage == 0:
                for item in bias_copies:
                    item.wait_recv()
                for item in [move(locals_[-1], bias.at[0]), move(outs[-1], bias.at[pl.ds(1, 3)])]:
                    item.wait()
            load(stage, 0)
        for item in loads[stage, s]:
            item.wait()
        if s < 3:
            load(stage, s + 1)
        streams = []
        for k in range(2):
            first, second = EARLY[stage][k]
            weight = blocks[2 * k].at[s % 2, pl.ds(0, outs[first].shape[1])]
            output = blocks[2 * k + 1].at[s % 2, pl.ds(0, outs[second].shape[1])]
            if first == second:
                output = weight
            at, count = places[2 * stage + k]
            offset = bias.at[s, :, pl.ds(at, count)]
            state = states[k] if stage == 0 else values_of[stage - 1][k][2]
            mine = values_of[stage][k]
            cut = [
                item.at[:, pl.ds(s * (item.shape[1] // 4), item.shape[1] // 4)] for item in mine[:2]
            ]
            ins = (state, weight, output, offset, rows[2 * stage + k])
            streams.append((ins, [*cut, *mine[2:]]))
        Step.now = s
        if stage == 1:
            ffn_kernel((), (), streams)
        else:
            mix_kernel(jobs[stage // 2], ids, streams)
        Step.now = None
        if s == 3:
            for k in range(10 * stage, 10 * stage + 10):
                finished.append(move(values[k], results[k]))

    tasks = {FIRST_TASK[stage] + s: (stage, s) for stage in range(3) for s in range(4)}
    from_x, from_y, low, high = [], [], [], []
    for step in range(max(len(segments) + 2, max(tasks) + 1)):
        if step < len(segments):
            segment = segments[step]
            for item in arrivals[step]:
                item.wait_recv()
            from_x.append(pass_on(segment, 0, across))
            from_y.append(pass_on(segment, 0, along))
            late[stage_of[segment[0]]].append(pass_on(segment, 0, core))
        if 0 <= step - 1 < len(segments):
            segment = segments[step - 1]
            from_x[step - 1].wait_recv()
            low.append(pass_on(segment, 2, along, 0, 0))
            from_y[step - 1].wait_recv()
            high.append(pass_on(segment, 4, across, 1, 1))
            late[stage_of[segment[0]]].append(pass_on(segment, 2, core))
            late[stage_of[segment[0]]].append(pass_on(segment, 4, core))
        if 0 <= step - 2 < len(segments):
            segment = segments[step - 2]
            low[step - 2].wait_recv()
            high[step - 2].wait_recv()
            late[stage_of[segment[0]]].append(pass_on(segment, 6, core))
        if step in tasks:
            run(*tasks[step])
    for item in late[3]:
        item.wait_recv()
    for item in copies:
        item.wait_send()
    for item in finished:
        item.wait()


def gather(stages, row, states, rows, ids, jobs, places):
    mats = [item for stage in stages for item in stage]
    stage_of = [k for k, stage in enumerate(stages) for _ in stage]
    segments = segments_of(mats)
    inputs = [local for local, _ in mats] + [row]
    weights = [jax.ShapeDtypeStruct((4,) + local.shape, bf16) for local, _ in mats]
    weights.append(jax.ShapeDtypeStruct((3,) + row.shape, bf16))
    shapes = early_outs(jobs, [count for _, count in places], states)
    results = [jax.ShapeDtypeStruct(shape, dtype) for shape, dtype in shapes]
    anywhere, near = pl.BlockSpec(memory_space=pl.ANY), pl.BlockSpec(memory_space=pltpu.VMEM)
    total = 12 * len(segments) + len(mats) + 3
    tops = [
        (max(inputs[EARLY[stage][k][part]].shape[0] for stage in range(3)), states[k].shape[1])
        for k in range(2)
        for part in range(2)
    ]
    found = pl.pallas_call(
        functools.partial(gather_kernel, segments, stage_of, len(mats), jobs, places, shapes),
        out_shape=weights + results,
        in_specs=[anywhere] * len(inputs) + [near] * 12,
        out_specs=[anywhere] * (len(weights) + len(results)),
        scratch_shapes=[pltpu.VMEM(shape, dtype) for shape, dtype in shapes]
        + [pltpu.VMEM((2,) + top, bf16) for top in tops]
        + [pltpu.VMEM((4,) + row.shape, bf16)]
        + [pltpu.SemaphoreType.DMA((total,))] * 2
        + [pltpu.SemaphoreType.DMA((48 + 30 + 2,))],
        compiler_params=pltpu.CompilerParams(collective_id=0, has_side_effects=True),
        name="gather",
    )(*inputs, *states, *rows, *ids)
    whole = [out.reshape(-1, out.shape[2]) for out in found[: len(mats)]]
    values = found[len(weights) :]
    return whole, found[len(mats)], [values[5 * k : 5 * k + 5] for k in range(6)]


def gather_plain(stages, row):
    tensor = lax.axis_size("tensor")
    whole = [
        jnp.concatenate([local] + [swap(local, "tensor", s) for s in range(1, tensor)])
        for stage in stages
        for local, _ in stage
    ]
    return whole, jnp.stack([swap(row, "tensor", s) for s in range(1, tensor)])


def wide(value):
    return value.astype(f32)


def reduce_plain(chunks, lefts, rights):
    tensor = lax.axis_size("tensor")
    done = []
    for _, terms in chunks:
        blocks = []
        for s in range(tensor):
            total = 0
            for left, right, column in terms:
                first = s * (rights[right].shape[1] // tensor) + column
                total = total + outer_sum(
                    lefts[left].astype(bf16), rights[right][:, first : first + LANES]
                )
            blocks.append(total)
        mine = lax.psum_scatter(
            jnp.stack(blocks, axis=1).astype(bf16), "dp", scatter_dimension=0, tiled=True
        )
        summed = wide(mine[:, 0])
        for s in range(1, tensor):
            summed = summed + wide(swap(mine[:, s], "tensor", s))
        done.append(summed)
    return jnp.concatenate(done)


TILE = 32
RING = 6


def backward_kernel(stages, counts, places, n_weights, *refs):
    n = len(stages)
    weights, refs = refs[:n_weights], refs[n_weights:]
    saved, refs = refs[: 10 * n], refs[10 * n :]
    uppers_in, rows, ids, refs = refs[:2], refs[2 : 2 + 2 * n], refs[2 + 2 * n : 6 + 2 * n], refs[6 + 2 * n :]
    final, refs = refs[:n], refs[n:]
    deltas, bias_out, sums_out, refs = refs[:2], refs[2], refs[3:5], refs[5:]
    landed, refs = refs[: 4 * n], refs[4 * n :]
    core_in, square_in, turn_in, line_in = (landed[k * n : (k + 1) * n] for k in range(4))
    reduce_scratch, refs = refs[:11], refs[11:]
    (
        own_buffer,
        core_out,
        core_buffer,
        kept,
        square_out,
        square_buffer,
        turn_out,
        turn_buffer,
        line_out,
        line_buffer,
        sums,
    ) = reduce_scratch
    small, small_in, bias_in, refs = refs[:3], refs[3:6], refs[6], refs[7:]
    blocks, refs = refs[:4], refs[4:]
    hidden_block, mixed_block, refs = refs[:2], refs[2:4], refs[4:]
    normed, scales, upstream, branch, refs = refs[:2], refs[2:4], refs[4:6], refs[6:8], refs[8:]
    states, first_right, second_right, refs = refs[:2], refs[2:4], refs[4:6], refs[6:]
    picked, turned, upper_block, refs = refs[:4], refs[4:6], refs[6:10], refs[10:]
    send_sems, recv_sems, local_sems = refs
    me, place_t = lax.axis_index("dp"), lax.axis_index("tensor")
    lines = [{"tensor": jnp.bitwise_xor(place_t, s)} for s in range(1, 4)]
    core, across, along = [{"dp": jnp.bitwise_xor(me, mask)} for mask in (1, 2, 4)]
    greet(lines + [core, across, along])
    remote, local = [], []

    def send(source, target, device):
        k = len(remote)
        item = pltpu.make_async_remote_copy(
            source, target, send_sems.at[k], recv_sems.at[k], device_id=device, device_id_type=MESH
        )
        item.start()
        remote.append(item)
        return item

    def move(source, target):
        item = pltpu.make_async_copy(source, target, local_sems.at[len(local)])
        item.start()
        local.append(item)
        return item

    def each_tile(count, body):
        def step(index, carry):
            body(pl.ds(pl.multiple_of(index * TILE, TILE), TILE))
            return carry

        lax.fori_loop(0, count // TILE, step, 0)

    pairs = [(stage, i) for stage in range(n) for i in range(2)]
    core_sends, square_sends, turn_sends, line_sends = {}, {}, {}, {}

    def saved_of(stage, k):
        return saved[(2 * stage + k) * 5 : (2 * stage + k + 1) * 5]

    start_loads, block_loads, slope_loads = {}, {}, {}

    def block_ref(stage, k):
        wide_kind = stages[stage][0] == "ffn"
        ref = (hidden_block if wide_kind else mixed_block)[k]
        return ref, saved_of(stage, k)[0].shape[1] // 4

    def load_block(stage, s):
        items = []
        for k in range(2):
            first, second = stages[stage][2][k]
            for part, index in ((0, first), (1, second)):
                if part and first == second:
                    continue
                source = weights[index]
                items.append(move(source.at[s], blocks[2 * k + part].at[pl.ds(0, source.shape[1])]))
            ref, width = block_ref(stage, k)
            source = saved_of(stage, k)[0]
            items.append(move(source.at[:, pl.ds(s * width, width)], ref.at[:, pl.ds(0, width)]))
        block_loads[stage, s] = items

    def load_start(stage):
        items = []
        for k in range(2):
            items.append(move(saved_of(stage, k)[1], normed[k]))
            items.append(move(saved_of(stage, k)[2], scales[k]))
        start_loads[stage] = items
        load_block(stage, 0)

    def load_slopes(stage):
        items = []
        for k in range(2):
            source = saved_of(stage, k)[3]
            items.append(move(source, second_right[k].at[:, pl.ds(0, source.shape[1])]))
            items.append(move(saved_of(stage, k)[4], states[k]))
        slope_loads[stage] = items

    def back(stage, s):
        kind, jobs, indices, norm, _ = stages[stage]
        if s == 0:
            for item in start_loads[stage]:
                item.wait()
        for item in block_loads[stage, s]:
            item.wait()
        streams = []
        for k in range(2):
            first, second = indices[k]
            weight = blocks[2 * k].at[pl.ds(0, weights[first].shape[1])]
            other = blocks[2 * k + 1].at[pl.ds(0, weights[second].shape[1])]
            if first == second:
                other = weight
            ref, width = block_ref(stage, k)
            at, count = places[2 * norm + k]
            ins = (upstream[k], normed[k], scales[k], rows[2 * stage + k], ref.at[:, pl.ds(0, width)])
            outs = [
                upstream[k],
                branch[k],
                small[1 + k].at[norm],
                first_right[k].at[:, pl.ds(s * width, width)],
                small[0].at[s, :, pl.ds(at, count)],
            ]
            if kind == "mix":
                size, heads = jobs[k][2], jobs[k][3]
                outs.append(upper_block[2 * (stage // 2) + k])
            streams.append(((*ins, weight, other), outs))
        Step.now = s
        if kind == "ffn":
            ffn_back_kernel((), (), streams)
        else:
            mix_back_kernel(jobs, ids, streams)
        Step.now = None
        if s < 3:
            load_block(stage, s + 1)
        elif stage + 1 < n:
            load_start(stage + 1)

    def produce(pair):
        stage, i = pairs[pair]
        if i == 0:
            for item in slope_loads[stage]:
                item.wait()
            for index, left in enumerate((states[0], branch[0], states[1], branch[1])):
                whole, target = turned[index // 2], picked[index]
                count = target.shape[0] // 8
                whole[...] = wide(left[...]).T.astype(bf16)
                for q in range(8):
                    owner = jnp.bitwise_xor(me, 2 * (q % 4) + q // 4)
                    first = pl.multiple_of(owner * count, 32)
                    target[q * count : (q + 1) * count, :] = whole[pl.ds(first, count), :]
        rights = (first_right[0], second_right[0], first_right[1], second_right[1])
        for half in range(2):
            slot, at = (2 * pair + half) % 4, 0
            if pair >= 2:
                core_sends[pair - 2, half].wait_send()
            for count, repeat, terms in stages[stage][4]:

                def chunk(index, carry):
                    total = None
                    for left, width, column in terms:
                        base = (2 * half + i) * width + column
                        part = pl.ds(pl.multiple_of(base + index * LANES, LANES), LANES)
                        term = jnp.dot(
                            picked[left][...], rights[left][:, part], preferred_element_type=f32
                        )
                        total = term if total is None else total + term
                    to = pl.ds(pl.multiple_of(at + index * count, 32), count)
                    for q in range(8):
                        minor = q % 4
                        place_q = 2 * (minor % 2) + minor // 2 if half == 0 else minor
                        target = core_out if q >= 4 else own_buffer
                        target[slot, place_q, to, :] = total[q * count : (q + 1) * count, :].astype(bf16)
                    return carry

                if repeat == 1:
                    chunk(0, 0)
                else:
                    lax.fori_loop(0, repeat, chunk, 0)
                at += count * repeat
            core_sends[pair, half] = send(
                core_out.at[slot, :, pl.ds(0, counts[stage])], core_in[stage].at[half, :, i], core
            )

    def slot_of(pair, half):
        return (2 * pair + half) % RING

    def square(pair):
        stage, i = pairs[pair]
        count, loads = counts[stage], []
        for half in range(2):
            core_sends[pair, half].wait_recv()
            loads.append(
                move(core_in[stage].at[half, :, i], core_buffer.at[half, :, pl.ds(0, count)])
            )
        for half in range(2):
            loads[half].wait()
            at, buffer = slot_of(pair, half), (2 * pair + half) % 4

            def body(tile):
                for q in range(4):
                    value = wide(own_buffer[buffer, q, tile, :]) + wide(core_buffer[half, q, tile, :])
                    target = kept if q < 2 else square_out
                    target[at, q % 2, tile, :] = value.astype(bf16)

            if pair >= RING // 2:
                square_sends[pair - RING // 2, half].wait_send()
            each_tile(count, body)
            square_sends[pair, half] = send(
                square_out.at[at, :, pl.ds(0, count)],
                square_in[stage].at[half, i],
                along if half else across,
            )

    def turn(pair):
        stage, i = pairs[pair]
        count, loads = counts[stage], []
        for half in range(2):
            square_sends[pair, half].wait_recv()
            loads.append(move(square_in[stage].at[half, i], square_buffer.at[half, :, pl.ds(0, count)]))
        for half in range(2):
            loads[half].wait()
            at = slot_of(pair, half)

            def body(tile):
                first = wide(kept[at, 0, tile, :]) + wide(square_buffer[half, 0, tile, :])
                kept[at, 0, tile, :] = first.astype(bf16)
                second = wide(kept[at, 1, tile, :]) + wide(square_buffer[half, 1, tile, :])
                turn_out[at, tile, :] = second.astype(bf16)

            if pair >= RING // 2:
                turn_sends[pair - RING // 2, half].wait_send()
            each_tile(count, body)
            turn_sends[pair, half] = send(
                turn_out.at[at, pl.ds(0, count)],
                turn_in[stage].at[half, i],
                across if half else along,
            )

    results = {}

    def line(pair):
        stage, i = pairs[pair]
        count, loads = counts[stage], []
        for half in range(2):
            turn_sends[pair, half].wait_recv()
            loads.append(move(turn_in[stage].at[half, i], turn_buffer.at[half, pl.ds(0, count)]))
        if i == 0 and stage >= 2:
            results[stage - 2].wait()
        for half in range(2):
            loads[half].wait()
            at, s = slot_of(pair, half), 2 * half + i

            def body(tile):
                value = wide(kept[at, 0, tile, :]) + wide(turn_buffer[half, tile, :])
                if s == 0:
                    sums[stage % 2, tile, :] = value
                else:
                    line_out[at, tile, :] = value.astype(bf16)

            if s and at in line_last:
                line_last.pop(at).wait_send()
            each_tile(count, body)
            if s:
                line_sends[pair, half] = send(
                    line_out.at[at, pl.ds(0, count)], line_in[stage].at[s - 1], lines[s - 1]
                )
                line_last[at] = line_sends[pair, half]

    line_last = {}

    def finish_stage(stage):
        count = counts[stage]
        for pair, half in ((2 * stage, 1), (2 * stage + 1, 0), (2 * stage + 1, 1)):
            line_sends[pair, half].wait_recv()
        move(line_in[stage], line_buffer.at[:, pl.ds(0, count)]).wait()

        def body(tile):
            value = sums[stage % 2, tile, :] + wide(line_buffer[0, tile, :])
            sums[stage % 2, tile, :] = (
                value + wide(line_buffer[1, tile, :]) + wide(line_buffer[2, tile, :])
            )

        each_tile(count, body)
        results[stage] = move(sums.at[stage % 2, pl.ds(0, count)], final[stage])

    small_sends, bias_sends = [], []
    steps = [core, across, along, lines[0], lines[1]]

    def small_step(k):
        if k:
            for index, item in enumerate(small_sends[k - 1]):
                item.wait_recv()
                item.wait_send()
                if item is not None:
                    arr = 3 - len(small_sends[k - 1]) + index
                    small[arr][...] = small[arr][...] + small_in[arr][k - 1]
        if k < 5:
            chosen = (0, 1, 2) if k < 3 else (1, 2)
            small_sends.append([send(small[arr], small_in[arr].at[k], steps[k]) for arr in chosen])
        if k == 3:
            for s in range(1, 4):
                bias_sends.append(send(small[0].at[s], bias_in.at[s - 1], lines[s - 1]))

    first_loads = [move(uppers_in[k], upstream[k]) for k in range(2)]
    load_start(0)
    load_slopes(0)
    for item in first_loads:
        item.wait()
    for s in range(4):
        back(0, s)
    produce(0)
    delta_moves = []
    for step in range(len(pairs) + 3):
        following = step // 2 + 1 if step % 2 == 0 and step // 2 + 1 < n else None
        if step < len(pairs):
            square(step)
            if step + 1 < len(pairs):
                produce(step + 1)
        if following is not None:
            load_slopes(following)
            back(following, 0)
            back(following, 1)
        if 0 <= step - 1 < len(pairs):
            turn(step - 1)
        if following is not None:
            back(following, 2)
        if 0 <= step - 2 < len(pairs):
            line(step - 2)
        if following is not None:
            back(following, 3)
        if following == n - 1:
            delta_moves += [move(upstream[k], deltas[k]) for k in range(2)]
        if step >= 3 and (step - 3) % 2:
            finish_stage((step - 3) // 2)
        if 0 <= step - 5 <= 5:
            small_step(step - 5)
    for item in bias_sends:
        item.wait_recv()
        item.wait_send()
    total = small[0][0]
    for k in range(3):
        total = total + bias_in[k]
    small[0][0] = total
    delta_moves.append(move(small[0].at[0], bias_out))
    delta_moves += [move(small[1 + k], sums_out[k]) for k in range(2)]
    for item in delta_moves + [results[n - 2], results[n - 1]]:
        item.wait()
    for group, lag in ((core_sends, 2), (square_sends, RING // 2), (turn_sends, RING // 2)):
        for (pair, half), item in group.items():
            if pair + lag >= len(pairs):
                item.wait_send()
    for item in line_last.values():
        item.wait_send()


def backward_all(stages, counts, places, weights, saved, uppers, rows, ids):
    n, top = len(stages), max(counts)
    anywhere, near = pl.BlockSpec(memory_space=pl.ANY), pl.BlockSpec(memory_space=pltpu.VMEM)
    landed = (
        [jax.ShapeDtypeStruct((2, 4, 2, count, LANES), bf16) for count in counts]
        + [jax.ShapeDtypeStruct((2, 2, 2, count, LANES), bf16) for count in counts]
        + [jax.ShapeDtypeStruct((2, 2, count, LANES), bf16) for count in counts]
        + [jax.ShapeDtypeStruct((3, count, LANES), bf16) for count in counts]
    )
    shapes = [item.shape for item in uppers]
    columns = sum(count for _, count in places)
    outs = [jax.ShapeDtypeStruct((count, LANES), f32) for count in counts]
    outs += [jax.ShapeDtypeStruct(shape, f32) for shape in shapes]
    outs.append(jax.ShapeDtypeStruct((1, columns), f32))
    outs += [jax.ShapeDtypeStruct((4, 3, shape[1]), f32) for shape in shapes]
    kinds = [stage[0] for stage in stages]

    def widest(position, k, kind=None):
        return max(
            saved[(2 * stage + k) * 5 + position].shape[1]
            for stage in range(n)
            if kind in (None, kinds[stage])
        )

    smalls = [(4, 1, columns)] + [(4, 3, shape[1]) for shape in shapes]
    scratch = [
        pltpu.VMEM((4, 4, top, LANES), bf16),
        pltpu.VMEM((4, 4, top, LANES), bf16),
        pltpu.VMEM((2, 4, top, LANES), bf16),
        pltpu.VMEM((RING, 2, top, LANES), bf16),
        pltpu.VMEM((RING, 2, top, LANES), bf16),
        pltpu.VMEM((2, 2, top, LANES), bf16),
        pltpu.VMEM((RING, top, LANES), bf16),
        pltpu.VMEM((2, top, LANES), bf16),
        pltpu.VMEM((RING, top, LANES), bf16),
        pltpu.VMEM((3, top, LANES), bf16),
        pltpu.VMEM((2, top, LANES), f32),
    ]
    scratch += [pltpu.VMEM(shape, f32) for shape in smalls]
    scratch += [pltpu.VMEM((5 if k else 3,) + shape, f32) for k, shape in enumerate(smalls)]
    scratch.append(pltpu.VMEM((3, 1, columns), f32))
    for k in range(2):
        for part in range(2):
            rows_max = max(
                weights[stage[2][k][part]].shape[1]
                for stage in stages
                if not (part and stage[2][k][0] == stage[2][k][1])
            )
            scratch.append(pltpu.VMEM((rows_max, shapes[k][1]), bf16))
    scratch += [pltpu.VMEM((shapes[k][0], widest(0, k, "ffn") // 4), f32) for k in range(2)]
    scratch += [pltpu.VMEM((shapes[k][0], widest(0, k, "mix") // 4), bf16) for k in range(2)]
    scratch += [pltpu.VMEM(shape, f32) for shape in shapes]
    scratch += [pltpu.VMEM((shape[0], 128), f32) for shape in shapes]
    scratch += [pltpu.VMEM(shape, f32) for shape in shapes]
    scratch += [pltpu.VMEM(shape, bf16) for shape in shapes]
    scratch += [pltpu.VMEM(shape, f32) for shape in shapes]
    scratch += [pltpu.VMEM((shapes[k][0], widest(0, k)), bf16) for k in range(2)]
    scratch += [pltpu.VMEM((shapes[k][0], widest(3, k)), bf16) for k in range(2)]
    scratch += [pltpu.VMEM(shapes[k // 2][::-1], bf16) for k in range(4)]
    scratch += [pltpu.VMEM(shape[::-1], bf16) for shape in shapes]
    for stage in (1, 3):
        for k in range(2):
            scratch.append(pltpu.VMEM((shapes[k][0], stages[stage][1][k][2] * stages[stage][1][k][3]), bf16))
    remote = 15 * n + 16
    scratch += [pltpu.SemaphoreType.DMA((remote,))] * 2 + [pltpu.SemaphoreType.DMA((64 * n,))]
    found = pl.pallas_call(
        functools.partial(backward_kernel, stages, counts, places, len(weights)),
        out_shape=outs + landed,
        in_specs=[anywhere] * (len(weights) + len(saved) + 2) + [near] * (2 * n + 4),
        out_specs=[anywhere] * (len(outs) + len(landed)),
        scratch_shapes=scratch,
        compiler_params=pltpu.CompilerParams(
            collective_id=1, has_side_effects=True, vmem_limit_bytes=67000000
        ),
        name="backward",
    )(*weights, *saved, *uppers, *rows, *ids)
    return found[:n], found[n : n + 2], found[n + 2], found[n + 3 : n + 5]


def split_packed(packed, layout):
    found, at = [], 0
    for rows, count, parts in layout:
        whole = jnp.concatenate(
            [packed[at + k * rows : at + (k + 1) * rows] for k in range(count)], axis=1
        )
        at += rows * count
        first = 0
        for kind, columns in parts:
            part = whole[:, first : first + columns]
            first += columns
            if kind == "cube":
                part = part.reshape(rows, 3, columns // 3)
            found.append(part.T if kind == "turn" else part)
    return found


def unpack_kernel(layouts, *refs):
    n = len(layouts)
    n_out = sum(len(parts) for layout in layouts for _, _, parts in layout)
    packed, outs, line = refs[:n], refs[n : n + n_out], refs[n + n_out]
    index = 0
    for source, layout in zip(packed, layouts):
        at = 0
        for rows, count, parts in layout:
            for k in range(count):
                line[:rows, k * LANES : (k + 1) * LANES] = source[at + k * rows : at + (k + 1) * rows, :]
            at += rows * count
            first = 0
            for kind, columns in parts:
                out = outs[index]
                if kind == "flat":
                    out[...] = line[:rows, first : first + columns]
                elif kind == "turn":
                    block = line[:rows, first : first + columns]
                    out[...] = block.T if rows % 128 == 0 else block
                else:
                    for k in range(3):
                        start = first + k * (columns // 3)
                        out[k, :, :] = line[:rows, start : start + columns // 3]
                index += 1
                first += columns


def unpack(packed, layouts):
    if lax.axis_size("dp") != 8:
        return [item for value, layout in zip(packed, layouts) for item in split_packed(value, layout)]
    shapes, top, widest = [], 0, 0
    for layout in layouts:
        for rows, count, parts in layout:
            top, widest = max(top, rows), max(widest, count * LANES)
            for kind, columns in parts:
                shapes.append(
                    {
                        "flat": (rows, columns),
                        "turn": (columns, rows) if rows % 128 == 0 else (rows, columns),
                        "cube": (3, rows, columns // 3),
                    }[kind]
                )
    found = pl.pallas_call(
        functools.partial(unpack_kernel, layouts),
        out_shape=[jax.ShapeDtypeStruct(shape, f32) for shape in shapes],
        scratch_shapes=[pltpu.VMEM((top, widest), f32)],
        name="unpack",
    )(*packed)
    kinds = [(kind, rows) for layout in layouts for rows, _, parts in layout for kind, _ in parts]
    return [
        item.transpose(1, 0, 2)
        if kind == "cube"
        else (item.T if kind == "turn" and rows % 128 else item)
        for item, (kind, rows) in zip(found, kinds)
    ]


def row_sum(value):
    return jnp.sum(wide(value), axis=0, keepdims=True)


class Step:
    now = None


def on_first(body):
    if Step.now is None:
        pl.when(pl.program_id(0) == 0)(body)
    elif Step.now == 0:
        body()


def on_later(body):
    if Step.now is None:
        pl.when(pl.program_id(0) > 0)(body)
    elif Step.now > 0:
        body()


def on_last(body):
    if Step.now is None:
        pl.when(pl.program_id(0) == pl.num_programs(0) - 1)(body)
    elif Step.now == 3:
        body()


def attend_probs(query, key, allowed, scale):
    scores = times_transpose(query, key) * scale
    scores = jnp.where(allowed, scores, -1e30)
    weights = jnp.exp(scores - jnp.max(scores, axis=1, keepdims=True))
    return weights / jnp.sum(weights, axis=1, keepdims=True)


def attend(jobs, mixed, ids, outs):
    for asks, gives, size, heads, shift in jobs:
        width = size * heads
        allowed = ids[2 * asks][...] == ids[2 * gives + 1][...]
        if shift:
            outs[asks][:, :shift] = jnp.zeros((outs[asks].shape[0], shift), bf16)
        for head in range(heads):
            at = head * size
            probs = attend_probs(
                mixed[asks][:, at : at + size],
                mixed[gives][:, width + at : width + at + size],
                allowed,
                1.0 / math.sqrt(size),
            )
            context = times(
                probs.astype(bf16), mixed[gives][:, 2 * width + at : 2 * width + at + size]
            )
            outs[asks][:, shift + at : shift + at + size] = context.astype(bf16)


def attend_back(jobs, mixed, ids, uppers, outs):
    for asks, gives, size, heads, shift in jobs:
        width = size * heads
        scale = 1.0 / math.sqrt(size)
        allowed = ids[2 * asks][...] == ids[2 * gives + 1][...]
        if shift:
            outs[asks][:, shift:] = jnp.zeros((outs[asks].shape[0], width), bf16)
        for head in range(heads):
            at = head * size
            query = mixed[asks][:, at : at + size]
            key = mixed[gives][:, width + at : width + at + size]
            value = mixed[gives][:, 2 * width + at : 2 * width + at + size]
            upper = uppers[asks][:, at : at + size]
            probs = attend_probs(query, key, allowed, scale)
            prob_delta = times_transpose(upper, value)
            inner = jnp.sum(prob_delta * probs, axis=1, keepdims=True)
            score_delta = (probs * (prob_delta - inner)).astype(bf16)
            outs[asks][:, at : at + size] = (times(score_delta, key) * scale).astype(bf16)
            outs[gives][:, width + at : width + at + size] = (
                outer_sum(score_delta, query) * scale
            ).astype(bf16)
            outs[gives][:, 2 * width + at : 2 * width + at + size] = outer_sum(
                probs.astype(bf16), upper
            ).astype(bf16)


def finish(state, total, rows, outs):
    branch = total[...] + rows[0:1, :]
    outs[0][...], outs[1][...], scale = norm_forward(
        wide(state[...]) + branch, rows[1:2, :], rows[2:3, :]
    )
    outs[2][...] = jnp.broadcast_to(scale, outs[2].shape)


def add_to(target, value):
    @on_first
    def _():
        target[...] = value

    @on_later
    def _():
        target[...] += value


def begin_back(upstream, saved, rows, outs):
    @on_first
    def _():
        upper, normed = upstream[...], saved[0][...]
        hidden_delta = norm_backward(upper, normed, saved[1][:, 0:1], rows[1:2, :])
        branch_delta = hidden_delta.astype(bf16)
        outs[0][...] = hidden_delta
        outs[1][...] = branch_delta
        outs[2][0:1, :] = row_sum(branch_delta)
        outs[2][1:2, :] = row_sum(upper * normed)
        outs[2][2:3, :] = row_sum(upper)


def mix_kernel(jobs, ids, streams):
    for (state, weight, output, offset, rows), (mixed, context, *final) in streams:
        mixed[...] = (times_transpose(state[...].astype(bf16), weight[...]) + wide(offset[...])).astype(bf16)
    attend(jobs, [out[0] for _, out in streams], ids, [out[1] for _, out in streams])
    for (asks, _, _, _, shift), (ins, outs) in zip(jobs, streams):
        state, output, rows = ins[0], ins[2], ins[4]
        add_to(outs[2], times(outs[1][:, shift:], output[shift:, :]))

        @on_last
        def _():
            finish(state, outs[2], rows, outs[2:])


def mix_back_kernel(jobs, ids, streams):
    for (asks, _, size, heads, shift), (ins, outs) in zip(jobs, streams):
        upstream, normed, scale, rows, mixed, weight, output = ins
        input_delta, branch_delta, sums, flat, bias, upper = outs
        begin_back(upstream, (normed, scale), rows, (input_delta, branch_delta, sums))
        upper[...] = times_transpose(branch_delta[...], output[shift:, :]).astype(bf16)
    attend_back(
        jobs,
        [ins[4] for ins, _ in streams],
        ids,
        [outs[5] for _, outs in streams],
        [outs[3] for _, outs in streams],
    )
    for (_, _, _, _, shift), (ins, outs) in zip(jobs, streams):
        width = shift or outs[3].shape[1]
        outs[4][...] = row_sum(outs[3][...])
        outs[0][...] += times(outs[3][:, :width], ins[5][:width, :])


def ffn_kernel(jobs, ids, streams):
    for (state, expand, reduce_weight, offset, rows), outs in streams:
        hidden, active, *final = outs
        value = times_transpose(state[...].astype(bf16), expand[...]) + wide(offset[...])
        hidden[...] = value
        active[...] = gelu_value(value).astype(bf16)
        add_to(final[0], times(active[...], reduce_weight[...]))

        @on_last
        def _():
            finish(state, final[0], rows, final)


def ffn_back_kernel(jobs, ids, streams):
    for ins, outs in streams:
        upstream, normed, scale, rows, hidden, expand, reduce_weight = ins
        input_delta, branch_delta, sums, inner, bias = outs
        begin_back(upstream, (normed, scale), rows, (input_delta, branch_delta, sums))
        active_delta = times_transpose(branch_delta[...], reduce_weight[...])
        inner[...] = (active_delta * gelu_slope(hidden[...])).astype(bf16)
        bias[...] = row_sum(inner[...])
        input_delta[...] += times(inner[...], expand[...])


def stage_kernel(body, jobs, n_ids, n_ins, n_outs, n_scratch, *refs):
    ids, at, streams = refs[:n_ids], n_ids, []
    n = len(refs[n_ids:]) // 2
    total_in, total_out = 2 * n_ins, 2 * n_outs
    ins = refs[n_ids : n_ids + total_in]
    outs = refs[n_ids + total_in : n_ids + total_in + total_out]
    scratch = refs[n_ids + total_in + total_out :]
    for k in range(2):
        streams.append(
            (
                ins[k * n_ins : (k + 1) * n_ins],
                [
                    *outs[k * n_outs : (k + 1) * n_outs],
                    *scratch[k * n_scratch : (k + 1) * n_scratch],
                ],
            )
        )
    body(jobs, ids, streams)


def run_stage(body, name, jobs, ids, streams, scratch=((), ())):
    steps = lax.axis_size("tensor")

    def spec(shape, how):
        if how is None:
            return pl.BlockSpec(shape, lambda s: (0, 0))
        block = tuple(size // steps if k == how else size for k, size in enumerate(shape))
        return pl.BlockSpec(block, (lambda s: (s, 0)) if how == 0 else (lambda s: (0, s)))

    ins = [item for stream in streams for item in stream[0]]
    outs = [item for stream in streams for item in stream[1]]
    found = pl.pallas_call(
        functools.partial(
            stage_kernel, body, jobs, len(ids), len(streams[0][0]), len(streams[0][1]), len(scratch[0])
        ),
        grid=(steps,),
        out_shape=[jax.ShapeDtypeStruct(shape, dtype) for shape, dtype, _ in outs],
        in_specs=[spec(item.shape, None) for item in ids]
        + [spec(item.shape, how) for item, how in ins],
        out_specs=[spec(shape, how) for shape, _, how in outs],
        scratch_shapes=[pltpu.VMEM(shape, bf16) for group in scratch for shape in group],
        cost_estimate=pl.CostEstimate(flops=0, bytes_accessed=0, transcendentals=0),
        name=name,
    )(*ids, *[item for item, _ in ins])
    half = len(streams[0][1])
    return found[:half], found[half:]


def final_shapes(state):
    return [(state.shape, f32, None), (state.shape, f32, None), ((state.shape[0], 128), f32, None)]


def mix_forward(name, jobs, ids, streams):
    tensor, groups = lax.axis_size("tensor"), []
    for (_, _, size, heads, shift), (state, weight, output, offset, rows) in zip(jobs, streams):
        ins = [(state, None), (weight, 0), (output, 0), (offset, 1), (rows, None)]
        tokens = state.shape[0]
        outs = [
            ((tokens, weight.shape[0]), bf16, 1),
            ((tokens, (shift + size * heads) * tensor), bf16, 1),
        ] + final_shapes(state)
        groups.append((ins, outs))
    return run_stage(mix_kernel, name, jobs, ids, groups)


def back_shapes(upstream, columns):
    tokens, width = upstream.shape
    return [
        (upstream.shape, f32, None),
        (upstream.shape, bf16, None),
        ((3, width), f32, None),
        ((tokens, columns), bf16, 1),
        ((1, columns), f32, 1),
    ]


def mix_backward(name, jobs, ids, streams):
    groups, scratch = [], []
    for (_, _, size, heads, _), (upstream, kept, weight, output, rows) in zip(jobs, streams):
        mixed, _, _, normed, scale = kept
        ins = [(upstream, None), (normed, None), (scale, None), (rows, None)]
        ins += [(mixed, 1), (weight, 0), (output, 0)]
        groups.append((ins, back_shapes(upstream, mixed.shape[1])))
        scratch.append([(upstream.shape[0], size * heads)])
    return run_stage(mix_back_kernel, name, jobs, ids, groups, scratch)


def ffn_forward(name, streams):
    groups = []
    for state, expand, reduce_weight, offset, rows in streams:
        ins = [(state, None), (expand, 0), (reduce_weight, 0), (offset, 1), (rows, None)]
        shape = (state.shape[0], expand.shape[0])
        groups.append((ins, [(shape, f32, 1), (shape, bf16, 1)] + final_shapes(state)))
    return run_stage(ffn_kernel, name, (), (), groups)


def ffn_backward(name, streams):
    groups = []
    for upstream, kept, expand, reduce_weight, rows in streams:
        hidden, _, _, normed, scale = kept
        ins = [(upstream, None), (normed, None), (scale, None), (rows, None)]
        ins += [(hidden, 1), (expand, 0), (reduce_weight, 0)]
        groups.append((ins, back_shapes(upstream, hidden.shape[1])))
    return run_stage(ffn_back_kernel, name, (), (), groups)


def bias_parts(sums, width):
    summed = sums.reshape(lax.axis_size("tensor"), -1)
    return jnp.stack([summed[:, :width], summed[:, 2 * width : 3 * width]], axis=1)


def plain_chunks(rows, left, width):
    return [(rows, [(left, left, at)]) for at in range(0, width, LANES)]


def per_device(
    text,
    image,
    text_segment,
    image_segment,
    text_cross_weight,
    text_cross_bias,
    text_cross_output,
    text_inner_expand,
    text_inner_offset,
    text_inner_reduce,
    text_self_weight,
    text_self_bias,
    text_self_output,
    text_outer_expand,
    text_outer_offset,
    text_outer_reduce,
    text_branch_bias,
    text_norm_gain,
    text_norm_shift,
    image_cross_weight,
    image_cross_bias,
    image_cross_output,
    image_inner_expand,
    image_inner_offset,
    image_inner_reduce,
    image_self_weight,
    image_self_bias,
    image_self_output,
    image_outer_expand,
    image_outer_offset,
    image_outer_reduce,
    image_branch_bias,
    image_norm_gain,
    image_norm_shift,
    text_cotangent,
    image_cotangent,
):
    tensor = lax.axis_size("tensor")
    place_t = lax.axis_index("tensor")
    dp = lax.axis_size("dp")
    count = text_segment.shape[0] // tensor
    captions = 4
    row_id = captions * jnp.arange(count, dtype=jnp.int32)[:, None]
    text_id = lax.dynamic_slice_in_dim(text_segment, place_t * count, count, 0) + row_id
    image_id = lax.dynamic_slice_in_dim(image_segment, place_t * count, count, 0) + row_id
    ids = [
        text_id.reshape(-1, 1),
        text_id.reshape(1, -1),
        image_id.reshape(-1, 1),
        image_id.reshape(1, -1),
    ]
    text_gain, text_shift = wide(text_norm_gain), wide(text_norm_shift)
    image_gain, image_shift = wide(image_norm_gain), wide(image_norm_shift)

    bias_order = (
        text_cross_bias,
        image_cross_bias,
        text_inner_offset,
        image_inner_offset,
        text_self_bias,
        image_self_bias,
        text_outer_offset,
        image_outer_offset,
    )
    def spread(bias, blank):
        zero = jnp.zeros_like(bias[0])
        return [bias[0], zero, bias[1]] + ([zero] if blank else [])

    bias_row = jnp.concatenate(
        [
            *spread(text_cross_bias, False),
            *spread(image_cross_bias, False),
            text_inner_offset,
            image_inner_offset,
            *spread(text_self_bias, True),
            *spread(image_self_bias, False),
            text_outer_offset,
            image_outer_offset,
        ]
    ).reshape(1, -1)
    places = early_columns(
        3 * text_cross_bias.shape[1],
        3 * image_cross_bias.shape[1],
        text_inner_offset.shape[0],
        image_inner_offset.shape[0],
        4 * text_self_bias.shape[1],
        3 * image_self_bias.shape[1],
    )

    def turned(weight):
        return weight.reshape(weight.shape[0], -1).T

    def single(*locals_):
        return [(local, [local.shape[0]]) for local in locals_]

    text_qkv = turned(text_self_weight)
    text_both = jnp.concatenate([text_qkv, text_self_output], axis=0)
    stages = [
        single(turned(text_cross_weight), text_cross_output, turned(image_cross_weight), image_cross_output),
        single(turned(text_inner_expand), text_inner_reduce, turned(image_inner_expand), image_inner_reduce),
        [(text_both, [text_qkv.shape[0], text_self_output.shape[0]])]
        + single(turned(image_self_weight), image_self_output),
        single(turned(text_outer_expand), text_outer_reduce, turned(image_outer_expand), image_outer_reduce),
    ]

    cross_jobs = [
        (0, 1, CO_DH, text_cross_output.shape[0] // CO_DH, 0),
        (1, 0, CO_DH, image_cross_output.shape[0] // CO_DH, 0),
    ]
    self_jobs = [
        (0, 0, TS_DH, text_self_output.shape[0] // TS_DH, 3 * text_self_output.shape[0]),
        (1, 1, VS_DH, image_self_output.shape[0] // VS_DH, 0),
    ]

    def rows_of(bias, gain, shift):
        return [jnp.stack([wide(bias[k]), gain[k], shift[k]]) for k in range(4)]

    text_rows = rows_of(text_branch_bias, text_gain, text_shift)
    image_rows = rows_of(image_branch_bias, image_gain, image_shift)
    if dp == 8:
        early_rows = [item for pair in zip(text_rows[:3], image_rows[:3]) for item in pair]
        gathered, bias_rows, early = gather(
            stages, bias_row, (text, image), early_rows, ids, (cross_jobs, self_jobs), places
        )
    else:
        gathered, bias_rows = gather_plain(stages, bias_row)
    text_cw, text_co, image_cw, image_co = gathered[:4]
    text_ie, text_ir, image_ie, image_ir = gathered[4:8]
    text_sb, image_sw, image_so = gathered[8:11]
    text_oe, text_or, image_oe, image_or = gathered[11:]
    bias_rows = jnp.concatenate([bias_row, bias_rows.reshape(tensor - 1, -1)], axis=0)
    offsets = [bias_rows[:, at : at + size].reshape(1, -1) for at, size in places]

    if dp == 8:
        text_cross, image_cross, text_inner, image_inner, text_self, image_self = early
    else:
        text_cross, image_cross = mix_forward(
            "cross",
            cross_jobs,
            ids,
            [
                (text, text_cw, text_co, offsets[0], text_rows[0]),
                (image, image_cw, image_co, offsets[1], image_rows[0]),
            ],
        )
        text_inner, image_inner = ffn_forward(
            "inner",
            [
                (text_cross[2], text_ie, text_ir, offsets[2], text_rows[1]),
                (image_cross[2], image_ie, image_ir, offsets[3], image_rows[1]),
            ],
        )
        text_self, image_self = mix_forward(
            "self",
            self_jobs,
            ids,
            [
                (text_inner[2], text_sb, text_sb, offsets[4], text_rows[2]),
                (image_inner[2], image_sw, image_so, offsets[5], image_rows[2]),
            ],
        )
    text_outer, image_outer = ffn_forward(
        "outer",
        [
            (text_self[2], text_oe, text_or, offsets[6], text_rows[3]),
            (image_self[2], image_oe, image_or, offsets[7], image_rows[3]),
        ],
    )
    text_result, image_result = text_outer[2], image_outer[2]

    text_part, image_part = text.shape[1] // dp, image.shape[1] // dp
    text_hidden, image_hidden = text_inner_offset.shape[0], image_inner_offset.shape[0]

    def ffn_reduction(states, backs, kepts):
        chunks = []
        for k in range(2):
            chunks += plain_chunks(text_part, k, text_hidden)
        for k in range(2):
            chunks += plain_chunks(image_part, 2 + k, image_hidden)
        lefts = [item for k in range(2) for item in (states[k], backs[k][1])]
        rights = [item for k in range(2) for item in (backs[k][3], kepts[k][1])]
        return chunks, lefts, rights

    def mix_reduction(states, backs, kepts, chunks):
        lefts = [item for k in range(2) for item in (states[k], backs[k][1])]
        rights = [item for k in range(2) for item in (backs[k][3], kepts[k][1])]
        return chunks, lefts, rights

    if dp == 8:
        qkv = 3 * text_self_output.shape[0]
        ffn_groups = [
            (text_part, text_hidden // LANES, [(0, text_hidden, 0)]),
            (text_part, text_hidden // LANES, [(1, text_hidden, 0)]),
            (image_part, image_hidden // LANES, [(2, image_hidden, 0)]),
            (image_part, image_hidden // LANES, [(3, image_hidden, 0)]),
        ]
        text_cols, image_cols = text_cross_output.shape[0], image_cross_output.shape[0]
        cross_groups = [
            (text_part, 3 * text_cols // LANES, [(0, 3 * text_cols, 0)]),
            (text_part, text_cols // LANES, [(1, text_cols, 0)]),
            (image_part, 3 * image_cols // LANES, [(2, 3 * image_cols, 0)]),
            (image_part, image_cols // LANES, [(3, image_cols, 0)]),
        ]
        both, plain_part = text_both.shape[0], qkv // LANES
        image_cols = image_self_output.shape[0]
        self_groups = [
            (text_part, plain_part, [(0, both, 0)]),
            (text_part, 1, [(0, both, plain_part * LANES), (1, both, plain_part * LANES)]),
            (image_part, 3 * image_cols // LANES, [(2, 3 * image_cols, 0)]),
            (image_part, image_cols // LANES, [(3, image_cols, 0)]),
        ]
        all_stages = [
            ("ffn", None, ((11, 12), (13, 14)), 3, ffn_groups),
            ("mix", self_jobs, ((8, 8), (9, 10)), 2, self_groups),
            ("ffn", None, ((4, 5), (6, 7)), 1, ffn_groups),
            ("mix", cross_jobs, ((0, 1), (2, 3)), 0, cross_groups),
        ]
        counts = [
            sum(count * repeat for count, repeat, _ in stage[4]) for stage in all_stages
        ]
        values = [(text_outer, image_outer), (text_self, image_self)]
        values += [(text_inner, image_inner), (text_cross, image_cross)]
        inputs = [(text_self[2], image_self[2]), (text_inner[2], image_inner[2])]
        inputs += [(text_cross[2], image_cross[2]), (wide(text), wide(image))]
        saved = []
        for pair, states in zip(values, inputs):
            for (columns, active, _, normed, scale), state in zip(pair, states):
                saved += [columns, normed, scale, active, state]
        back_rows = []
        for norm in (3, 2, 1, 0):
            back_rows += [text_rows[norm], image_rows[norm]]
        packed, (delta_text, delta_image), bias_sum, shared_sums = backward_all(
            all_stages,
            counts,
            places,
            [item.reshape(tensor, -1, item.shape[1]) for item in gathered],
            saved,
            (wide(text_cotangent), wide(image_cotangent)),
            back_rows,
            ids,
        )
    else:
        outer_back = ffn_backward(
            "outer_back",
            [
                (wide(text_cotangent), text_outer, text_oe, text_or, text_rows[3]),
                (wide(image_cotangent), image_outer, image_oe, image_or, image_rows[3]),
            ],
        )
        outer = ffn_reduction((text_self[2], image_self[2]), outer_back, (text_outer, image_outer))
        upstream = (outer_back[0][0], outer_back[1][0])

        self_back = mix_backward(
            "self_back",
            self_jobs,
            ids,
            [
                (upstream[0], text_self, text_sb, text_sb, text_rows[2]),
                (upstream[1], image_self, image_sw, image_so, image_rows[2]),
            ],
        )
        mixed_width = 3 * text_self_output.shape[0]
        chunks = []
        for at in range(0, text_both.shape[0], LANES):
            terms = [(0, 0, at)] if at < mixed_width else []
            if at + LANES > mixed_width:
                terms.append((1, 1, at))
            chunks.append((text_part, terms))
        chunks += plain_chunks(image_part, 2, 3 * image_self_output.shape[0])
        chunks += plain_chunks(image_part, 3, image_self_output.shape[0])
        own = mix_reduction((text_inner[2], image_inner[2]), self_back, (text_self, image_self), chunks)
        upstream = (self_back[0][0], self_back[1][0])

        inner_back = ffn_backward(
            "inner_back",
            [
                (upstream[0], text_inner, text_ie, text_ir, text_rows[1]),
                (upstream[1], image_inner, image_ie, image_ir, image_rows[1]),
            ],
        )
        inner = ffn_reduction((text_cross[2], image_cross[2]), inner_back, (text_inner, image_inner))
        upstream = (inner_back[0][0], inner_back[1][0])

        cross_back = mix_backward(
            "cross_back",
            cross_jobs,
            ids,
            [
                (upstream[0], text_cross, text_cw, text_co, text_rows[0]),
                (upstream[1], image_cross, image_cw, image_co, image_rows[0]),
            ],
        )
        delta_text, delta_image = cross_back[0][0], cross_back[1][0]
        chunks = plain_chunks(text_part, 0, 3 * text_cross_output.shape[0])
        chunks += plain_chunks(text_part, 1, text_cross_output.shape[0])
        chunks += plain_chunks(image_part, 2, 3 * image_cross_output.shape[0])
        chunks += plain_chunks(image_part, 3, image_cross_output.shape[0])
        cross = mix_reduction((text, image), cross_back, (text_cross, image_cross), chunks)
        backs = (cross_back, inner_back, self_back, outer_back)
        bias_deltas = (
            bias_parts(cross_back[0][4], text_cross_output.shape[0]),
            bias_parts(cross_back[1][4], image_cross_output.shape[0]),
            inner_back[0][4],
            inner_back[1][4],
            bias_parts(self_back[0][4], text_self_output.shape[0]),
            bias_parts(self_back[1][4], image_self_output.shape[0]),
            outer_back[0][4],
            outer_back[1][4],
        )
        by_near = jnp.concatenate([item.reshape(tensor, -1) for item in bias_deltas], axis=1)
        by_place = jnp.stack(
            [lax.dynamic_index_in_dim(by_near, place_t ^ s, 0, False) for s in range(tensor)]
        )
        shared = tuple(
            jnp.stack([back[k][2][kind] for back in backs]) for k in range(2) for kind in range(3)
        )
        line = jnp.concatenate([by_place.reshape(-1)] + [item.reshape(-1) for item in shared])
        line = line.reshape(-1, 128)
        packed = [reduce_plain(*item) for item in (outer, own, inner, cross)]
        line = lax.psum(line, ("dp", "tensor")).reshape(-1)
    text_wide, image_wide = text_cross_output.shape[0], image_cross_output.shape[0]
    text_own, image_own = text_self_output.shape[0], image_self_output.shape[0]
    ffn_layout = [
        (text_part, text_hidden // LANES, [("flat", text_hidden)]),
        (text_part, text_hidden // LANES, [("turn", text_hidden)]),
        (image_part, image_hidden // LANES, [("flat", image_hidden)]),
        (image_part, image_hidden // LANES, [("turn", image_hidden)]),
    ]
    own_layout = [
        (text_part, 4 * text_own // LANES, [("cube", 3 * text_own), ("turn", text_own)]),
        (image_part, 3 * image_own // LANES, [("cube", 3 * image_own)]),
        (image_part, image_own // LANES, [("turn", image_own)]),
    ]
    cross_layout = [
        (text_part, 3 * text_wide // LANES, [("cube", 3 * text_wide)]),
        (text_part, text_wide // LANES, [("turn", text_wide)]),
        (image_part, 3 * image_wide // LANES, [("cube", 3 * image_wide)]),
        (image_part, image_wide // LANES, [("turn", image_wide)]),
    ]
    layouts = [ffn_layout, own_layout, ffn_layout, cross_layout]
    deltas = unpack(packed, layouts)
    text_oe_delta, text_or_delta, image_oe_delta, image_or_delta = deltas[:4]
    text_sw_delta, text_so_delta, image_sw_delta, image_so_delta = deltas[4:8]
    text_ie_delta, text_ir_delta, image_ie_delta, image_ir_delta = deltas[8:12]
    text_cw_delta, text_co_delta, image_cw_delta, image_co_delta = deltas[12:]
    if dp == 8:
        pieces = [bias_sum[0, at : at + size] for at, size in places]
        bias_out = []
        for item, piece in zip(bias_order, pieces):
            if item.ndim == 2:
                width = item.shape[1]
                piece = jnp.stack([piece[:width], piece[2 * width : 3 * width]])
            bias_out.append(piece)
        shared_out = [value[:, kind] for value in shared_sums for kind in range(3)]
    else:
        by_place = lax.dynamic_index_in_dim(
            line[: by_place.size].reshape(by_place.shape), place_t, 0, False
        )
        bias_out, at = [], 0
        for item in bias_order:
            size = math.prod(item.shape)
            bias_out.append(by_place[at : at + size].reshape(item.shape))
            at += size
        shared_out, at = [], math.prod(by_near.shape)
        for item in shared:
            shared_out.append(line[at : at + item.size].reshape(item.shape))
            at += item.size

    return (
        text_result,
        image_result,
        delta_text,
        delta_image,
        text_cw_delta,
        bias_out[0],
        text_co_delta,
        text_ie_delta,
        bias_out[2],
        text_ir_delta,
        text_sw_delta,
        bias_out[4],
        text_so_delta,
        text_oe_delta,
        bias_out[6],
        text_or_delta,
        shared_out[0],
        shared_out[1],
        shared_out[2],
        image_cw_delta,
        bias_out[1],
        image_co_delta,
        image_ie_delta,
        bias_out[3],
        image_ir_delta,
        image_sw_delta,
        bias_out[5],
        image_so_delta,
        image_oe_delta,
        bias_out[7],
        image_or_delta,
        shared_out[3],
        shared_out[4],
        shared_out[5],
    )


def solution(mesh):
    placed = (
        P(("dp", "tensor"), None),
        P(("dp", "tensor"), None),
        P("dp", None),
        P("dp", None),
        P(None, None, "tensor"),
        P(None, "tensor"),
        P("tensor", None),
        P(None, "tensor"),
        P("tensor"),
        P("tensor", None),
        P(None, None, "tensor"),
        P(None, "tensor"),
        P("tensor", None),
        P(None, "tensor"),
        P("tensor"),
        P("tensor", None),
        P(),
        P(),
        P(),
        P(None, None, "tensor"),
        P(None, "tensor"),
        P("tensor", None),
        P(None, "tensor"),
        P("tensor"),
        P("tensor", None),
        P(None, None, "tensor"),
        P(None, "tensor"),
        P("tensor", None),
        P(None, "tensor"),
        P("tensor"),
        P("tensor", None),
        P(),
        P(),
        P(),
        P(("dp", "tensor"), None),
        P(("dp", "tensor"), None),
    )
    return jax.shard_map(
        per_device,
        mesh=mesh,
        in_specs=placed,
        out_specs=(
            P(("dp", "tensor"), None),
            P(("dp", "tensor"), None),
            P(("dp", "tensor"), None),
            P(("dp", "tensor"), None),
            P("dp", None, "tensor"),
            P(None, "tensor"),
            P("tensor", "dp"),
            P("dp", "tensor"),
            P("tensor"),
            P("tensor", "dp"),
            P("dp", None, "tensor"),
            P(None, "tensor"),
            P("tensor", "dp"),
            P("dp", "tensor"),
            P("tensor"),
            P("tensor", "dp"),
            P(),
            P(),
            P(),
            P("dp", None, "tensor"),
            P(None, "tensor"),
            P("tensor", "dp"),
            P("dp", "tensor"),
            P("tensor"),
            P("tensor", "dp"),
            P("dp", None, "tensor"),
            P(None, "tensor"),
            P("tensor", "dp"),
            P("dp", "tensor"),
            P("tensor"),
            P("tensor", "dp"),
            P(),
            P(),
            P(),
        ),
        check_vma=False,
    )
```

```python
import functools
import math

import jax
import jax.numpy as jnp
from jax import lax
from jax.experimental import pallas as pl
from jax.experimental.pallas import tpu as pltpu
from jax.sharding import PartitionSpec as P

CO_DH = 128
TS_DH = 64
VS_DH = 128
LANES = 256
MESH = pl.DeviceIdType.MESH

norm_eps = 1e-05
root_half = 0.7071067811865476
inv_root_tau = 0.3989422804014327
f32 = jnp.float32
bf16 = jnp.bfloat16


def gelu_value(hidden):
    return 0.5 * hidden * (1.0 + lax.erf(hidden * root_half))


def gelu_slope(hidden):
    return (
        0.5 * (1.0 + lax.erf(hidden * root_half))
        + hidden * jnp.exp(-0.5 * hidden * hidden) * inv_root_tau
    )


def norm_forward(hidden, gain, shift):
    center = hidden - jnp.mean(hidden, axis=1, keepdims=True)
    scale = lax.rsqrt(jnp.mean(center * center, axis=1, keepdims=True) + norm_eps)
    normed = center * scale
    return normed * gain + shift, normed, scale


def norm_backward(upstream, normed, scale, gain):
    inner = upstream * gain
    return scale * (
        inner
        - jnp.mean(inner, axis=1, keepdims=True)
        - normed * jnp.mean(inner * normed, axis=1, keepdims=True)
    )


def times(left, right):
    return jnp.dot(left, right, preferred_element_type=f32)


def times_transpose(left, right):
    return lax.dot_general(left, right, (((1,), (1,)), ((), ())), preferred_element_type=f32)


def outer_sum(left, right):
    return lax.dot_general(left, right, (((0,), (0,)), ((), ())), preferred_element_type=f32)


def swap(value, axis, mask):
    return lax.ppermute(value, axis, [(i, i ^ mask) for i in range(lax.axis_size(axis))])


def segments_of(mats):
    dp, found = lax.axis_size("dp"), []
    for index, (_, parts) in enumerate(mats):
        base = 0
        for total in parts:
            found.append((index, base, total // dp))
            base += total
    return found


def greet(partners):
    barrier = pltpu.get_barrier_semaphore()
    for partner in partners:
        pl.semaphore_signal(barrier, inc=1, device_id=partner, device_id_type=MESH)
    pl.semaphore_wait(barrier, len(partners))


EARLY = (((0, 1), (2, 3)), ((4, 5), (6, 7)), ((8, 8), (9, 10)))
FIRST_TASK = (6, 10, 14)


def early_columns(text_width, image_width, text_hidden, image_hidden, text_own, image_own):
    counts = [text_width, image_width, text_hidden, image_hidden, text_own, image_own]
    counts += [text_hidden, image_hidden]
    found, at = [], 0
    for count in counts:
        found.append((at, count))
        at += count
    return found


def early_outs(jobs, widths, states):
    outs = []
    for stage in range(3):
        for k, state in enumerate(states):
            tokens, width = state.shape
            if stage == 1:
                shapes = [((tokens, 4 * widths[2 + k]), f32), ((tokens, 4 * widths[2 + k]), bf16)]
            else:
                _, _, size, heads, shift = jobs[stage // 2][k]
                columns = (shift or 3 * size * heads) + (size * heads if shift else 0)
                shapes = [((tokens, 4 * columns), bf16), ((tokens, 4 * (shift + size * heads)), bf16)]
            shapes += [((tokens, width), f32), ((tokens, width), f32), ((tokens, 128), f32)]
            outs += shapes
    return outs


def gather_kernel(segments, stage_of, n_mats, jobs, places, shapes, *refs):
    n_in = n_mats + 1
    locals_, refs = refs[:n_in], refs[n_in:]
    states, rows, ids, refs = refs[:2], refs[2:8], refs[8:12], refs[12:]
    outs, refs = refs[:n_in], refs[n_in:]
    results, refs = refs[: len(shapes)], refs[len(shapes) :]
    values, refs = refs[: len(shapes)], refs[len(shapes) :]
    blocks, bias, (send_sems, recv_sems, local_sems) = refs[:4], refs[4], refs[5:]
    me, place_t = lax.axis_index("dp"), lax.axis_index("tensor")
    lines = [{"tensor": jnp.bitwise_xor(place_t, s)} for s in range(1, 4)]
    core, across, along = [{"dp": jnp.bitwise_xor(me, mask)} for mask in (1, 2, 4)]
    greet(lines + [core, across, along])
    copies, moves = [], []

    def copy(source, target, device):
        k = len(copies)
        item = pltpu.make_async_remote_copy(
            source, target, send_sems.at[k], recv_sems.at[k], device_id=device, device_id_type=MESH
        )
        item.start()
        copies.append(item)
        return item

    def move(source, target):
        item = pltpu.make_async_copy(source, target, local_sems.at[len(moves)])
        item.start()
        moves.append(item)
        return item

    def rows_of(segment, mask):
        _, base, count = segment
        return pl.ds(pl.multiple_of(base + jnp.bitwise_xor(me, mask) * count, 8), count)

    def pass_on(segment, mask, device, low=0, high=1):
        index = segment[0]
        width = outs[index].shape[2] // 2
        part = outs[index].at[
            pl.ds(1, 3), rows_of(segment, mask), pl.ds(low * width, (high + 1 - low) * width)
        ]
        return copy(part, part, device)

    late = [[] for _ in range(4)]
    bias_copies = [copy(locals_[-1], outs[-1].at[s], lines[s]) for s in range(3)]
    arrivals = []
    for segment in segments:
        index, part = segment[0], rows_of(segment, 0)
        arrivals.append(
            [copy(locals_[index].at[part], outs[index].at[s + 1, part], lines[s]) for s in range(3)]
        )
    for index in range(n_mats):
        late[stage_of[index]].append(copy(locals_[index], outs[index].at[0], core))

    loads, finished = {}, []
    values_of = [
        [values[(2 * stage + k) * 5 : (2 * stage + k + 1) * 5] for k in range(2)] for stage in range(3)
    ]

    def load(stage, s):
        slot, items = s % 2, []
        for k in range(2):
            for part in range(2):
                if part and EARLY[stage][k][0] == EARLY[stage][k][1]:
                    continue
                source = outs[EARLY[stage][k][part]]
                items.append(
                    move(source.at[s], blocks[2 * k + part].at[slot, pl.ds(0, source.shape[1])])
                )
        loads[stage, s] = items

    def run(stage, s):
        if s == 0:
            for item in late[stage]:
                item.wait_recv()
            if stage == 0:
                for item in bias_copies:
                    item.wait_recv()
                for item in [move(locals_[-1], bias.at[0]), move(outs[-1], bias.at[pl.ds(1, 3)])]:
                    item.wait()
            load(stage, 0)
        for item in loads[stage, s]:
            item.wait()
        if s < 3:
            load(stage, s + 1)
        streams = []
        for k in range(2):
            first, second = EARLY[stage][k]
            weight = blocks[2 * k].at[s % 2, pl.ds(0, outs[first].shape[1])]
            output = blocks[2 * k + 1].at[s % 2, pl.ds(0, outs[second].shape[1])]
            if first == second:
                output = weight
            at, count = places[2 * stage + k]
            offset = bias.at[s, :, pl.ds(at, count)]
            state = states[k] if stage == 0 else values_of[stage - 1][k][2]
            mine = values_of[stage][k]
            cut = [
                item.at[:, pl.ds(s * (item.shape[1] // 4), item.shape[1] // 4)] for item in mine[:2]
            ]
            ins = (state, weight, output, offset, rows[2 * stage + k])
            streams.append((ins, [*cut, *mine[2:]]))
        Step.now = s
        if stage == 1:
            ffn_kernel((), (), streams)
        else:
            mix_kernel(jobs[stage // 2], ids, streams)
        Step.now = None
        if s == 3:
            for k in range(10 * stage, 10 * stage + 10):
                finished.append(move(values[k], results[k]))

    tasks = {FIRST_TASK[stage] + s: (stage, s) for stage in range(3) for s in range(4)}
    from_x, from_y, low, high = [], [], [], []
    for step in range(max(len(segments) + 2, max(tasks) + 1)):
        if step < len(segments):
            segment = segments[step]
            for item in arrivals[step]:
                item.wait_recv()
            from_x.append(pass_on(segment, 0, across))
            from_y.append(pass_on(segment, 0, along))
            late[stage_of[segment[0]]].append(pass_on(segment, 0, core))
        if 0 <= step - 1 < len(segments):
            segment = segments[step - 1]
            from_x[step - 1].wait_recv()
            low.append(pass_on(segment, 2, along, 0, 0))
            from_y[step - 1].wait_recv()
            high.append(pass_on(segment, 4, across, 1, 1))
            late[stage_of[segment[0]]].append(pass_on(segment, 2, core))
            late[stage_of[segment[0]]].append(pass_on(segment, 4, core))
        if 0 <= step - 2 < len(segments):
            segment = segments[step - 2]
            low[step - 2].wait_recv()
            high[step - 2].wait_recv()
            late[stage_of[segment[0]]].append(pass_on(segment, 6, core))
        if step in tasks:
            run(*tasks[step])
    for item in late[3]:
        item.wait_recv()
    for item in copies:
        item.wait_send()
    for item in finished:
        item.wait()


def gather(stages, row, states, rows, ids, jobs, places):
    mats = [item for stage in stages for item in stage]
    stage_of = [k for k, stage in enumerate(stages) for _ in stage]
    segments = segments_of(mats)
    inputs = [local for local, _ in mats] + [row]
    weights = [jax.ShapeDtypeStruct((4,) + local.shape, bf16) for local, _ in mats]
    weights.append(jax.ShapeDtypeStruct((3,) + row.shape, bf16))
    shapes = early_outs(jobs, [count for _, count in places], states)
    results = [jax.ShapeDtypeStruct(shape, dtype) for shape, dtype in shapes]
    anywhere, near = pl.BlockSpec(memory_space=pl.ANY), pl.BlockSpec(memory_space=pltpu.VMEM)
    total = 12 * len(segments) + len(mats) + 3
    tops = [
        (max(inputs[EARLY[stage][k][part]].shape[0] for stage in range(3)), states[k].shape[1])
        for k in range(2)
        for part in range(2)
    ]
    found = pl.pallas_call(
        functools.partial(gather_kernel, segments, stage_of, len(mats), jobs, places, shapes),
        out_shape=weights + results,
        in_specs=[anywhere] * len(inputs) + [near] * 12,
        out_specs=[anywhere] * (len(weights) + len(results)),
        scratch_shapes=[pltpu.VMEM(shape, dtype) for shape, dtype in shapes]
        + [pltpu.VMEM((2,) + top, bf16) for top in tops]
        + [pltpu.VMEM((4,) + row.shape, bf16)]
        + [pltpu.SemaphoreType.DMA((total,))] * 2
        + [pltpu.SemaphoreType.DMA((48 + 30 + 2,))],
        compiler_params=pltpu.CompilerParams(collective_id=0, has_side_effects=True),
        name="gather",
    )(*inputs, *states, *rows, *ids)
    whole = [out.reshape(-1, out.shape[2]) for out in found[: len(mats)]]
    values = found[len(weights) :]
    return whole, found[len(mats)], [values[5 * k : 5 * k + 5] for k in range(6)]


def gather_plain(stages, row):
    tensor = lax.axis_size("tensor")
    whole = [
        jnp.concatenate([local] + [swap(local, "tensor", s) for s in range(1, tensor)])
        for stage in stages
        for local, _ in stage
    ]
    return whole, jnp.stack([swap(row, "tensor", s) for s in range(1, tensor)])


def wide(value):
    return value.astype(f32)


def reduce_plain(chunks, lefts, rights):
    tensor = lax.axis_size("tensor")
    done = []
    for _, terms in chunks:
        blocks = []
        for s in range(tensor):
            total = 0
            for left, right, column in terms:
                first = s * (rights[right].shape[1] // tensor) + column
                total = total + outer_sum(
                    lefts[left].astype(bf16), rights[right][:, first : first + LANES]
                )
            blocks.append(total)
        mine = lax.psum_scatter(
            jnp.stack(blocks, axis=1).astype(bf16), "dp", scatter_dimension=0, tiled=True
        )
        summed = wide(mine[:, 0])
        for s in range(1, tensor):
            summed = summed + wide(swap(mine[:, s], "tensor", s))
        done.append(summed)
    return jnp.concatenate(done)


TILE = 32
RING = 6


def backward_kernel(stages, counts, places, n_weights, *refs):
    n = len(stages)
    weights, refs = refs[:n_weights], refs[n_weights:]
    saved, refs = refs[: 10 * n], refs[10 * n :]
    uppers_in, rows, ids, refs = refs[:2], refs[2 : 2 + 2 * n], refs[2 + 2 * n : 6 + 2 * n], refs[6 + 2 * n :]
    final, refs = refs[:n], refs[n:]
    deltas, bias_out, sums_out, refs = refs[:2], refs[2], refs[3:5], refs[5:]
    landed, refs = refs[: 4 * n], refs[4 * n :]
    core_in, square_in, turn_in, line_in = (landed[k * n : (k + 1) * n] for k in range(4))
    reduce_scratch, refs = refs[:11], refs[11:]
    (
        own_buffer,
        core_out,
        core_buffer,
        kept,
        square_out,
        square_buffer,
        turn_out,
        turn_buffer,
        line_out,
        line_buffer,
        sums,
    ) = reduce_scratch
    small, small_in, bias_in, refs = refs[:3], refs[3:6], refs[6], refs[7:]
    blocks, refs = refs[:4], refs[4:]
    hidden_block, mixed_block, refs = refs[:2], refs[2:4], refs[4:]
    normed, scales, upstream, branch, refs = refs[:2], refs[2:4], refs[4:6], refs[6:8], refs[8:]
    states, first_right, second_right, refs = refs[:2], refs[2:4], refs[4:6], refs[6:]
    picked, turned, upper_block, refs = refs[:4], refs[4:6], refs[6:10], refs[10:]
    send_sems, recv_sems, local_sems = refs
    me, place_t = lax.axis_index("dp"), lax.axis_index("tensor")
    lines = [{"tensor": jnp.bitwise_xor(place_t, s)} for s in range(1, 4)]
    core, across, along = [{"dp": jnp.bitwise_xor(me, mask)} for mask in (1, 2, 4)]
    greet(lines + [core, across, along])
    remote, local = [], []

    def send(source, target, device):
        k = len(remote)
        item = pltpu.make_async_remote_copy(
            source, target, send_sems.at[k], recv_sems.at[k], device_id=device, device_id_type=MESH
        )
        item.start()
        remote.append(item)
        return item

    def move(source, target):
        item = pltpu.make_async_copy(source, target, local_sems.at[len(local)])
        item.start()
        local.append(item)
        return item

    def each_tile(count, body):
        def step(index, carry):
            body(pl.ds(pl.multiple_of(index * TILE, TILE), TILE))
            return carry

        lax.fori_loop(0, count // TILE, step, 0)

    pairs = [(stage, i) for stage in range(n) for i in range(2)]
    core_sends, square_sends, turn_sends, line_sends = {}, {}, {}, {}

    def saved_of(stage, k):
        return saved[(2 * stage + k) * 5 : (2 * stage + k + 1) * 5]

    start_loads, block_loads, slope_loads = {}, {}, {}

    def block_ref(stage, k):
        wide_kind = stages[stage][0] == "ffn"
        ref = (hidden_block if wide_kind else mixed_block)[k]
        return ref, saved_of(stage, k)[0].shape[1] // 4

    def load_block(stage, s):
        items = []
        for k in range(2):
            first, second = stages[stage][2][k]
            for part, index in ((0, first), (1, second)):
                if part and first == second:
                    continue
                source = weights[index]
                items.append(move(source.at[s], blocks[2 * k + part].at[pl.ds(0, source.shape[1])]))
            ref, width = block_ref(stage, k)
            source = saved_of(stage, k)[0]
            items.append(move(source.at[:, pl.ds(s * width, width)], ref.at[:, pl.ds(0, width)]))
        block_loads[stage, s] = items

    def load_start(stage):
        items = []
        for k in range(2):
            items.append(move(saved_of(stage, k)[1], normed[k]))
            items.append(move(saved_of(stage, k)[2], scales[k]))
        start_loads[stage] = items
        load_block(stage, 0)

    def load_slopes(stage):
        items = []
        for k in range(2):
            source = saved_of(stage, k)[3]
            items.append(move(source, second_right[k].at[:, pl.ds(0, source.shape[1])]))
            items.append(move(saved_of(stage, k)[4], states[k]))
        slope_loads[stage] = items

    def back(stage, s):
        kind, jobs, indices, norm, _ = stages[stage]
        if s == 0:
            for item in start_loads[stage]:
                item.wait()
        for item in block_loads[stage, s]:
            item.wait()
        streams = []
        for k in range(2):
            first, second = indices[k]
            weight = blocks[2 * k].at[pl.ds(0, weights[first].shape[1])]
            other = blocks[2 * k + 1].at[pl.ds(0, weights[second].shape[1])]
            if first == second:
                other = weight
            ref, width = block_ref(stage, k)
            at, count = places[2 * norm + k]
            ins = (upstream[k], normed[k], scales[k], rows[2 * stage + k], ref.at[:, pl.ds(0, width)])
            outs = [
                upstream[k],
                branch[k],
                small[1 + k].at[norm],
                first_right[k].at[:, pl.ds(s * width, width)],
                small[0].at[s, :, pl.ds(at, count)],
            ]
            if kind == "mix":
                size, heads = jobs[k][2], jobs[k][3]
                outs.append(upper_block[2 * (stage // 2) + k])
            streams.append(((*ins, weight, other), outs))
        Step.now = s
        if kind == "ffn":
            ffn_back_kernel((), (), streams)
        else:
            mix_back_kernel(jobs, ids, streams)
        Step.now = None
        if s < 3:
            load_block(stage, s + 1)
        elif stage + 1 < n:
            load_start(stage + 1)

    def produce(pair):
        stage, i = pairs[pair]
        if i == 0:
            for item in slope_loads[stage]:
                item.wait()
            for index, left in enumerate((states[0], branch[0], states[1], branch[1])):
                whole, target = turned[index // 2], picked[index]
                count = target.shape[0] // 8
                whole[...] = wide(left[...]).T.astype(bf16)
                for q in range(8):
                    owner = jnp.bitwise_xor(me, 2 * (q % 4) + q // 4)
                    first = pl.multiple_of(owner * count, 32)
                    target[q * count : (q + 1) * count, :] = whole[pl.ds(first, count), :]
        rights = (first_right[0], second_right[0], first_right[1], second_right[1])
        for half in range(2):
            slot, at = (2 * pair + half) % 4, 0
            if pair >= 2:
                core_sends[pair - 2, half].wait_send()
            for count, repeat, terms in stages[stage][4]:

                def chunk(index, carry):
                    total = None
                    for left, width, column in terms:
                        base = (2 * half + i) * width + column
                        part = pl.ds(pl.multiple_of(base + index * LANES, LANES), LANES)
                        term = jnp.dot(
                            picked[left][...], rights[left][:, part], preferred_element_type=f32
                        )
                        total = term if total is None else total + term
                    to = pl.ds(pl.multiple_of(at + index * count, 32), count)
                    for q in range(8):
                        minor = q % 4
                        place_q = 2 * (minor % 2) + minor // 2 if half == 0 else minor
                        target = core_out if q >= 4 else own_buffer
                        target[slot, place_q, to, :] = total[q * count : (q + 1) * count, :].astype(bf16)
                    return carry

                if repeat == 1:
                    chunk(0, 0)
                else:
                    lax.fori_loop(0, repeat, chunk, 0)
                at += count * repeat
            core_sends[pair, half] = send(
                core_out.at[slot, :, pl.ds(0, counts[stage])], core_in[stage].at[half, :, i], core
            )

    def slot_of(pair, half):
        return (2 * pair + half) % RING

    def square(pair):
        stage, i = pairs[pair]
        count, loads = counts[stage], []
        for half in range(2):
            core_sends[pair, half].wait_recv()
            loads.append(
                move(core_in[stage].at[half, :, i], core_buffer.at[half, :, pl.ds(0, count)])
            )
        for half in range(2):
            loads[half].wait()
            at, buffer = slot_of(pair, half), (2 * pair + half) % 4

            def body(tile):
                for q in range(4):
                    value = wide(own_buffer[buffer, q, tile, :]) + wide(core_buffer[half, q, tile, :])
                    target = kept if q < 2 else square_out
                    target[at, q % 2, tile, :] = value.astype(bf16)

            if pair >= RING // 2:
                square_sends[pair - RING // 2, half].wait_send()
            each_tile(count, body)
            square_sends[pair, half] = send(
                square_out.at[at, :, pl.ds(0, count)],
                square_in[stage].at[half, i],
                along if half else across,
            )

    def turn(pair):
        stage, i = pairs[pair]
        count, loads = counts[stage], []
        for half in range(2):
            square_sends[pair, half].wait_recv()
            loads.append(move(square_in[stage].at[half, i], square_buffer.at[half, :, pl.ds(0, count)]))
        for half in range(2):
            loads[half].wait()
            at = slot_of(pair, half)

            def body(tile):
                first = wide(kept[at, 0, tile, :]) + wide(square_buffer[half, 0, tile, :])
                kept[at, 0, tile, :] = first.astype(bf16)
                second = wide(kept[at, 1, tile, :]) + wide(square_buffer[half, 1, tile, :])
                turn_out[at, tile, :] = second.astype(bf16)

            if pair >= RING // 2:
                turn_sends[pair - RING // 2, half].wait_send()
            each_tile(count, body)
            turn_sends[pair, half] = send(
                turn_out.at[at, pl.ds(0, count)],
                turn_in[stage].at[half, i],
                across if half else along,
            )

    results = {}

    def line(pair):
        stage, i = pairs[pair]
        count, loads = counts[stage], []
        for half in range(2):
            turn_sends[pair, half].wait_recv()
            loads.append(move(turn_in[stage].at[half, i], turn_buffer.at[half, pl.ds(0, count)]))
        if i == 0 and stage >= 2:
            results[stage - 2].wait()
        for half in range(2):
            loads[half].wait()
            at, s = slot_of(pair, half), 2 * half + i

            def body(tile):
                value = wide(kept[at, 0, tile, :]) + wide(turn_buffer[half, tile, :])
                if s == 0:
                    sums[stage % 2, tile, :] = value
                else:
                    line_out[at, tile, :] = value.astype(bf16)

            if s and at in line_last:
                line_last.pop(at).wait_send()
            each_tile(count, body)
            if s:
                line_sends[pair, half] = send(
                    line_out.at[at, pl.ds(0, count)], line_in[stage].at[s - 1], lines[s - 1]
                )
                line_last[at] = line_sends[pair, half]

    line_last = {}

    def finish_stage(stage):
        count = counts[stage]
        for pair, half in ((2 * stage, 1), (2 * stage + 1, 0), (2 * stage + 1, 1)):
            line_sends[pair, half].wait_recv()
        move(line_in[stage], line_buffer.at[:, pl.ds(0, count)]).wait()

        def body(tile):
            value = sums[stage % 2, tile, :] + wide(line_buffer[0, tile, :])
            sums[stage % 2, tile, :] = (
                value + wide(line_buffer[1, tile, :]) + wide(line_buffer[2, tile, :])
            )

        each_tile(count, body)
        results[stage] = move(sums.at[stage % 2, pl.ds(0, count)], final[stage])

    small_sends, bias_sends = [], []
    steps = [core, across, along, lines[0], lines[1]]

    def small_step(k):
        if k:
            for index, item in enumerate(small_sends[k - 1]):
                item.wait_recv()
                item.wait_send()
                if item is not None:
                    arr = 3 - len(small_sends[k - 1]) + index
                    small[arr][...] = small[arr][...] + small_in[arr][k - 1]
        if k < 5:
            chosen = (0, 1, 2) if k < 3 else (1, 2)
            small_sends.append([send(small[arr], small_in[arr].at[k], steps[k]) for arr in chosen])
        if k == 3:
            for s in range(1, 4):
                bias_sends.append(send(small[0].at[s], bias_in.at[s - 1], lines[s - 1]))

    first_loads = [move(uppers_in[k], upstream[k]) for k in range(2)]
    load_start(0)
    load_slopes(0)
    for item in first_loads:
        item.wait()
    for s in range(4):
        back(0, s)
    produce(0)
    delta_moves = []
    for step in range(len(pairs) + 3):
        following = step // 2 + 1 if step % 2 == 0 and step // 2 + 1 < n else None
        if step < len(pairs):
            square(step)
            if step % 2 and step + 1 < len(pairs):
                back(step // 2 + 1, 3)
                if step // 2 + 1 == n - 1:
                    delta_moves += [move(upstream[k], deltas[k]) for k in range(2)]
            if step + 1 < len(pairs):
                produce(step + 1)
        if following is not None:
            load_slopes(following)
            back(following, 0)
            back(following, 1)
        if 0 <= step - 1 < len(pairs):
            turn(step - 1)
        if following is not None:
            back(following, 2)
        if 0 <= step - 2 < len(pairs):
            line(step - 2)
        if step >= 3 and (step - 3) % 2:
            finish_stage((step - 3) // 2)
        if 0 <= step - 5 <= 5:
            small_step(step - 5)
    for item in bias_sends:
        item.wait_recv()
        item.wait_send()
    total = small[0][0]
    for k in range(3):
        total = total + bias_in[k]
    small[0][0] = total
    delta_moves.append(move(small[0].at[0], bias_out))
    delta_moves += [move(small[1 + k], sums_out[k]) for k in range(2)]
    for item in delta_moves + [results[n - 2], results[n - 1]]:
        item.wait()
    for group, lag in ((core_sends, 2), (square_sends, RING // 2), (turn_sends, RING // 2)):
        for (pair, half), item in group.items():
            if pair + lag >= len(pairs):
                item.wait_send()
    for item in line_last.values():
        item.wait_send()


def backward_all(stages, counts, places, weights, saved, uppers, rows, ids):
    n, top = len(stages), max(counts)
    anywhere, near = pl.BlockSpec(memory_space=pl.ANY), pl.BlockSpec(memory_space=pltpu.VMEM)
    landed = (
        [jax.ShapeDtypeStruct((2, 4, 2, count, LANES), bf16) for count in counts]
        + [jax.ShapeDtypeStruct((2, 2, 2, count, LANES), bf16) for count in counts]
        + [jax.ShapeDtypeStruct((2, 2, count, LANES), bf16) for count in counts]
        + [jax.ShapeDtypeStruct((3, count, LANES), bf16) for count in counts]
    )
    shapes = [item.shape for item in uppers]
    columns = sum(count for _, count in places)
    outs = [jax.ShapeDtypeStruct((count, LANES), f32) for count in counts]
    outs += [jax.ShapeDtypeStruct(shape, f32) for shape in shapes]
    outs.append(jax.ShapeDtypeStruct((1, columns), f32))
    outs += [jax.ShapeDtypeStruct((4, 3, shape[1]), f32) for shape in shapes]
    kinds = [stage[0] for stage in stages]

    def widest(position, k, kind=None):
        return max(
            saved[(2 * stage + k) * 5 + position].shape[1]
            for stage in range(n)
            if kind in (None, kinds[stage])
        )

    smalls = [(4, 1, columns)] + [(4, 3, shape[1]) for shape in shapes]
    scratch = [
        pltpu.VMEM((4, 4, top, LANES), bf16),
        pltpu.VMEM((4, 4, top, LANES), bf16),
        pltpu.VMEM((2, 4, top, LANES), bf16),
        pltpu.VMEM((RING, 2, top, LANES), bf16),
        pltpu.VMEM((RING, 2, top, LANES), bf16),
        pltpu.VMEM((2, 2, top, LANES), bf16),
        pltpu.VMEM((RING, top, LANES), bf16),
        pltpu.VMEM((2, top, LANES), bf16),
        pltpu.VMEM((RING, top, LANES), bf16),
        pltpu.VMEM((3, top, LANES), bf16),
        pltpu.VMEM((2, top, LANES), f32),
    ]
    scratch += [pltpu.VMEM(shape, f32) for shape in smalls]
    scratch += [pltpu.VMEM((5 if k else 3,) + shape, f32) for k, shape in enumerate(smalls)]
    scratch.append(pltpu.VMEM((3, 1, columns), f32))
    for k in range(2):
        for part in range(2):
            rows_max = max(
                weights[stage[2][k][part]].shape[1]
                for stage in stages
                if not (part and stage[2][k][0] == stage[2][k][1])
            )
            scratch.append(pltpu.VMEM((rows_max, shapes[k][1]), bf16))
    scratch += [pltpu.VMEM((shapes[k][0], widest(0, k, "ffn") // 4), f32) for k in range(2)]
    scratch += [pltpu.VMEM((shapes[k][0], widest(0, k, "mix") // 4), bf16) for k in range(2)]
    scratch += [pltpu.VMEM(shape, f32) for shape in shapes]
    scratch += [pltpu.VMEM((shape[0], 128), f32) for shape in shapes]
    scratch += [pltpu.VMEM(shape, f32) for shape in shapes]
    scratch += [pltpu.VMEM(shape, bf16) for shape in shapes]
    scratch += [pltpu.VMEM(shape, f32) for shape in shapes]
    scratch += [pltpu.VMEM((shapes[k][0], widest(0, k)), bf16) for k in range(2)]
    scratch += [pltpu.VMEM((shapes[k][0], widest(3, k)), bf16) for k in range(2)]
    scratch += [pltpu.VMEM(shapes[k // 2][::-1], bf16) for k in range(4)]
    scratch += [pltpu.VMEM(shape[::-1], bf16) for shape in shapes]
    for stage in (1, 3):
        for k in range(2):
            scratch.append(pltpu.VMEM((shapes[k][0], stages[stage][1][k][2] * stages[stage][1][k][3]), bf16))
    remote = 15 * n + 16
    scratch += [pltpu.SemaphoreType.DMA((remote,))] * 2 + [pltpu.SemaphoreType.DMA((64 * n,))]
    found = pl.pallas_call(
        functools.partial(backward_kernel, stages, counts, places, len(weights)),
        out_shape=outs + landed,
        in_specs=[anywhere] * (len(weights) + len(saved) + 2) + [near] * (2 * n + 4),
        out_specs=[anywhere] * (len(outs) + len(landed)),
        scratch_shapes=scratch,
        compiler_params=pltpu.CompilerParams(
            collective_id=1, has_side_effects=True, vmem_limit_bytes=67000000
        ),
        name="backward",
    )(*weights, *saved, *uppers, *rows, *ids)
    return found[:n], found[n : n + 2], found[n + 2], found[n + 3 : n + 5]


def split_packed(packed, layout):
    found, at = [], 0
    for rows, count, parts in layout:
        whole = jnp.concatenate(
            [packed[at + k * rows : at + (k + 1) * rows] for k in range(count)], axis=1
        )
        at += rows * count
        first = 0
        for kind, columns in parts:
            part = whole[:, first : first + columns]
            first += columns
            if kind == "cube":
                part = part.reshape(rows, 3, columns // 3)
            found.append(part.T if kind == "turn" else part)
    return found


def unpack_kernel(layouts, smalls, *refs):
    n = len(layouts)
    n_out = sum(len(parts) for layout in layouts for _, _, parts in layout)
    packed, (bias_sum, *shared), refs = refs[:n], refs[n : n + 3], refs[n + 3 :]
    outs, small_outs, line = refs[:n_out], refs[n_out:-1], refs[-1]
    for out, (at, _, paired) in zip(small_outs, smalls):
        width = out.shape[1]
        out[0:1, :] = bias_sum[:, at : at + width]
        if paired:
            out[1:2, :] = bias_sum[:, at + 2 * width : at + 3 * width]
    for index, out in enumerate(small_outs[len(smalls) :]):
        for k in range(4):
            out[k : k + 1, :] = shared[index // 3][k, index % 3 : index % 3 + 1, :]
    index = 0
    for source, layout in zip(packed, layouts):
        at = 0
        for rows, count, parts in layout:
            for k in range(count):
                line[:rows, k * LANES : (k + 1) * LANES] = source[at + k * rows : at + (k + 1) * rows, :]
            at += rows * count
            first = 0
            for kind, columns in parts:
                out = outs[index]
                if kind == "flat":
                    out[...] = line[:rows, first : first + columns]
                elif kind == "turn":
                    block = line[:rows, first : first + columns]
                    out[...] = block.T if rows % 128 == 0 else block
                else:
                    for k in range(3):
                        start = first + k * (columns // 3)
                        out[k, :, :] = line[:rows, start : start + columns // 3]
                index += 1
                first += columns


def unpack(packed, layouts, smalls=(), sums=()):
    if lax.axis_size("dp") != 8:
        return [item for value, layout in zip(packed, layouts) for item in split_packed(value, layout)]
    shapes, top, widest = [], 0, 0
    for layout in layouts:
        for rows, count, parts in layout:
            top, widest = max(top, rows), max(widest, count * LANES)
            for kind, columns in parts:
                shapes.append(
                    {
                        "flat": (rows, columns),
                        "turn": (columns, rows) if rows % 128 == 0 else (rows, columns),
                        "cube": (3, rows, columns // 3),
                    }[kind]
                )
    found = pl.pallas_call(
        functools.partial(unpack_kernel, layouts, smalls),
        out_shape=[
            jax.ShapeDtypeStruct(shape, f32)
            for shape in shapes
            + [(2 if paired else 1, width) for _, width, paired in smalls]
            + [(4, value.shape[2]) for value in sums[1:] for _ in range(3)]
        ],
        scratch_shapes=[pltpu.VMEM((top, widest), f32)],
        name="unpack",
    )(*packed, *sums)
    kinds = [(kind, rows) for layout in layouts for rows, _, parts in layout for kind, _ in parts]
    return [
        item.transpose(1, 0, 2)
        if kind == "cube"
        else (item.T if kind == "turn" and rows % 128 else item)
        for item, (kind, rows) in zip(found, kinds)
    ] + list(found[len(kinds) :])


def row_sum(value):
    return jnp.sum(wide(value), axis=0, keepdims=True)


class Step:
    now = None


def on_first(body):
    if Step.now is None:
        pl.when(pl.program_id(0) == 0)(body)
    elif Step.now == 0:
        body()


def on_later(body):
    if Step.now is None:
        pl.when(pl.program_id(0) > 0)(body)
    elif Step.now > 0:
        body()


def on_last(body):
    if Step.now is None:
        pl.when(pl.program_id(0) == pl.num_programs(0) - 1)(body)
    elif Step.now == 3:
        body()


def attend_probs(query, key, allowed, scale):
    scores = times_transpose(query, key) * scale
    scores = jnp.where(allowed, scores, -1e30)
    weights = jnp.exp(scores - jnp.max(scores, axis=1, keepdims=True))
    return weights / jnp.sum(weights, axis=1, keepdims=True)


def attend(jobs, mixed, ids, outs):
    for asks, gives, size, heads, shift in jobs:
        width = size * heads
        allowed = ids[2 * asks][...] == ids[2 * gives + 1][...]
        if shift:
            outs[asks][:, :shift] = jnp.zeros((outs[asks].shape[0], shift), bf16)
        for head in range(heads):
            at = head * size
            probs = attend_probs(
                mixed[asks][:, at : at + size],
                mixed[gives][:, width + at : width + at + size],
                allowed,
                1.0 / math.sqrt(size),
            )
            context = times(
                probs.astype(bf16), mixed[gives][:, 2 * width + at : 2 * width + at + size]
            )
            outs[asks][:, shift + at : shift + at + size] = context.astype(bf16)


def attend_back(jobs, mixed, ids, uppers, outs):
    for asks, gives, size, heads, shift in jobs:
        width = size * heads
        scale = 1.0 / math.sqrt(size)
        allowed = ids[2 * asks][...] == ids[2 * gives + 1][...]
        if shift:
            outs[asks][:, shift:] = jnp.zeros((outs[asks].shape[0], width), bf16)
        for head in range(heads):
            at = head * size
            query = mixed[asks][:, at : at + size]
            key = mixed[gives][:, width + at : width + at + size]
            value = mixed[gives][:, 2 * width + at : 2 * width + at + size]
            upper = uppers[asks][:, at : at + size]
            probs = attend_probs(query, key, allowed, scale)
            prob_delta = times_transpose(upper, value)
            inner = jnp.sum(prob_delta * probs, axis=1, keepdims=True)
            score_delta = (probs * (prob_delta - inner)).astype(bf16)
            outs[asks][:, at : at + size] = (times(score_delta, key) * scale).astype(bf16)
            outs[gives][:, width + at : width + at + size] = (
                outer_sum(score_delta, query) * scale
            ).astype(bf16)
            outs[gives][:, 2 * width + at : 2 * width + at + size] = outer_sum(
                probs.astype(bf16), upper
            ).astype(bf16)


def finish(state, total, rows, outs):
    branch = total[...] + rows[0:1, :]
    outs[0][...], outs[1][...], scale = norm_forward(
        wide(state[...]) + branch, rows[1:2, :], rows[2:3, :]
    )
    outs[2][...] = jnp.broadcast_to(scale, outs[2].shape)


def add_to(target, value):
    @on_first
    def _():
        target[...] = value

    @on_later
    def _():
        target[...] += value


def begin_back(upstream, saved, rows, outs):
    @on_first
    def _():
        upper, normed = upstream[...], saved[0][...]
        hidden_delta = norm_backward(upper, normed, saved[1][:, 0:1], rows[1:2, :])
        branch_delta = hidden_delta.astype(bf16)
        outs[0][...] = hidden_delta
        outs[1][...] = branch_delta
        outs[2][0:1, :] = row_sum(branch_delta)
        outs[2][1:2, :] = row_sum(upper * normed)
        outs[2][2:3, :] = row_sum(upper)


def mix_kernel(jobs, ids, streams):
    for (state, weight, output, offset, rows), (mixed, context, *final) in streams:
        mixed[...] = (times_transpose(state[...].astype(bf16), weight[...]) + wide(offset[...])).astype(bf16)
    attend(jobs, [out[0] for _, out in streams], ids, [out[1] for _, out in streams])
    for (asks, _, _, _, shift), (ins, outs) in zip(jobs, streams):
        state, output, rows = ins[0], ins[2], ins[4]
        add_to(outs[2], times(outs[1][:, shift:], output[shift:, :]))

        @on_last
        def _():
            finish(state, outs[2], rows, outs[2:])


def mix_back_kernel(jobs, ids, streams):
    for (asks, _, size, heads, shift), (ins, outs) in zip(jobs, streams):
        upstream, normed, scale, rows, mixed, weight, output = ins
        input_delta, branch_delta, sums, flat, bias, upper = outs
        begin_back(upstream, (normed, scale), rows, (input_delta, branch_delta, sums))
        upper[...] = times_transpose(branch_delta[...], output[shift:, :]).astype(bf16)
    attend_back(
        jobs,
        [ins[4] for ins, _ in streams],
        ids,
        [outs[5] for _, outs in streams],
        [outs[3] for _, outs in streams],
    )
    for (_, _, _, _, shift), (ins, outs) in zip(jobs, streams):
        width = shift or outs[3].shape[1]
        outs[4][...] = row_sum(outs[3][...])
        outs[0][...] += times(outs[3][:, :width], ins[5][:width, :])


def ffn_kernel(jobs, ids, streams):
    for (state, expand, reduce_weight, offset, rows), outs in streams:
        hidden, active, *final = outs
        value = times_transpose(state[...].astype(bf16), expand[...]) + wide(offset[...])
        hidden[...] = value
        active[...] = gelu_value(value).astype(bf16)
        add_to(final[0], times(active[...], reduce_weight[...]))

        @on_last
        def _():
            finish(state, final[0], rows, final)


def ffn_back_kernel(jobs, ids, streams):
    for ins, outs in streams:
        upstream, normed, scale, rows, hidden, expand, reduce_weight = ins
        input_delta, branch_delta, sums, inner, bias = outs
        begin_back(upstream, (normed, scale), rows, (input_delta, branch_delta, sums))
        active_delta = times_transpose(branch_delta[...], reduce_weight[...])
        inner[...] = (active_delta * gelu_slope(hidden[...])).astype(bf16)
        bias[...] = row_sum(inner[...])
        input_delta[...] += times(inner[...], expand[...])


def stage_kernel(body, jobs, n_ids, n_ins, n_outs, n_scratch, *refs):
    ids, at, streams = refs[:n_ids], n_ids, []
    n = len(refs[n_ids:]) // 2
    total_in, total_out = 2 * n_ins, 2 * n_outs
    ins = refs[n_ids : n_ids + total_in]
    outs = refs[n_ids + total_in : n_ids + total_in + total_out]
    scratch = refs[n_ids + total_in + total_out :]
    for k in range(2):
        streams.append(
            (
                ins[k * n_ins : (k + 1) * n_ins],
                [
                    *outs[k * n_outs : (k + 1) * n_outs],
                    *scratch[k * n_scratch : (k + 1) * n_scratch],
                ],
            )
        )
    body(jobs, ids, streams)


def run_stage(body, name, jobs, ids, streams, scratch=((), ())):
    steps = lax.axis_size("tensor")

    def spec(shape, how):
        if how is None:
            return pl.BlockSpec(shape, lambda s: (0, 0))
        block = tuple(size // steps if k == how else size for k, size in enumerate(shape))
        return pl.BlockSpec(block, (lambda s: (s, 0)) if how == 0 else (lambda s: (0, s)))

    ins = [item for stream in streams for item in stream[0]]
    outs = [item for stream in streams for item in stream[1]]
    found = pl.pallas_call(
        functools.partial(
            stage_kernel, body, jobs, len(ids), len(streams[0][0]), len(streams[0][1]), len(scratch[0])
        ),
        grid=(steps,),
        out_shape=[jax.ShapeDtypeStruct(shape, dtype) for shape, dtype, _ in outs],
        in_specs=[spec(item.shape, None) for item in ids]
        + [spec(item.shape, how) for item, how in ins],
        out_specs=[spec(shape, how) for shape, _, how in outs],
        scratch_shapes=[pltpu.VMEM(shape, bf16) for group in scratch for shape in group],
        cost_estimate=pl.CostEstimate(flops=0, bytes_accessed=0, transcendentals=0),
        name=name,
    )(*ids, *[item for item, _ in ins])
    half = len(streams[0][1])
    return found[:half], found[half:]


def final_shapes(state):
    return [(state.shape, f32, None), (state.shape, f32, None), ((state.shape[0], 128), f32, None)]


def mix_forward(name, jobs, ids, streams):
    tensor, groups = lax.axis_size("tensor"), []
    for (_, _, size, heads, shift), (state, weight, output, offset, rows) in zip(jobs, streams):
        ins = [(state, None), (weight, 0), (output, 0), (offset, 1), (rows, None)]
        tokens = state.shape[0]
        outs = [
            ((tokens, weight.shape[0]), bf16, 1),
            ((tokens, (shift + size * heads) * tensor), bf16, 1),
        ] + final_shapes(state)
        groups.append((ins, outs))
    return run_stage(mix_kernel, name, jobs, ids, groups)


def back_shapes(upstream, columns):
    tokens, width = upstream.shape
    return [
        (upstream.shape, f32, None),
        (upstream.shape, bf16, None),
        ((3, width), f32, None),
        ((tokens, columns), bf16, 1),
        ((1, columns), f32, 1),
    ]


def mix_backward(name, jobs, ids, streams):
    groups, scratch = [], []
    for (_, _, size, heads, _), (upstream, kept, weight, output, rows) in zip(jobs, streams):
        mixed, _, _, normed, scale = kept
        ins = [(upstream, None), (normed, None), (scale, None), (rows, None)]
        ins += [(mixed, 1), (weight, 0), (output, 0)]
        groups.append((ins, back_shapes(upstream, mixed.shape[1])))
        scratch.append([(upstream.shape[0], size * heads)])
    return run_stage(mix_back_kernel, name, jobs, ids, groups, scratch)


def ffn_forward(name, streams):
    groups = []
    for state, expand, reduce_weight, offset, rows in streams:
        ins = [(state, None), (expand, 0), (reduce_weight, 0), (offset, 1), (rows, None)]
        shape = (state.shape[0], expand.shape[0])
        groups.append((ins, [(shape, f32, 1), (shape, bf16, 1)] + final_shapes(state)))
    return run_stage(ffn_kernel, name, (), (), groups)


def ffn_backward(name, streams):
    groups = []
    for upstream, kept, expand, reduce_weight, rows in streams:
        hidden, _, _, normed, scale = kept
        ins = [(upstream, None), (normed, None), (scale, None), (rows, None)]
        ins += [(hidden, 1), (expand, 0), (reduce_weight, 0)]
        groups.append((ins, back_shapes(upstream, hidden.shape[1])))
    return run_stage(ffn_back_kernel, name, (), (), groups)


def bias_parts(sums, width):
    summed = sums.reshape(lax.axis_size("tensor"), -1)
    return jnp.stack([summed[:, :width], summed[:, 2 * width : 3 * width]], axis=1)


def plain_chunks(rows, left, width):
    return [(rows, [(left, left, at)]) for at in range(0, width, LANES)]


def per_device(
    text,
    image,
    text_segment,
    image_segment,
    text_cross_weight,
    text_cross_bias,
    text_cross_output,
    text_inner_expand,
    text_inner_offset,
    text_inner_reduce,
    text_self_weight,
    text_self_bias,
    text_self_output,
    text_outer_expand,
    text_outer_offset,
    text_outer_reduce,
    text_branch_bias,
    text_norm_gain,
    text_norm_shift,
    image_cross_weight,
    image_cross_bias,
    image_cross_output,
    image_inner_expand,
    image_inner_offset,
    image_inner_reduce,
    image_self_weight,
    image_self_bias,
    image_self_output,
    image_outer_expand,
    image_outer_offset,
    image_outer_reduce,
    image_branch_bias,
    image_norm_gain,
    image_norm_shift,
    text_cotangent,
    image_cotangent,
):
    tensor = lax.axis_size("tensor")
    place_t = lax.axis_index("tensor")
    dp = lax.axis_size("dp")
    count = text_segment.shape[0] // tensor
    captions = 4
    row_id = captions * jnp.arange(count, dtype=jnp.int32)[:, None]
    text_id = lax.dynamic_slice_in_dim(text_segment, place_t * count, count, 0) + row_id
    image_id = lax.dynamic_slice_in_dim(image_segment, place_t * count, count, 0) + row_id
    ids = [
        text_id.reshape(-1, 1),
        text_id.reshape(1, -1),
        image_id.reshape(-1, 1),
        image_id.reshape(1, -1),
    ]
    text_gain, text_shift = wide(text_norm_gain), wide(text_norm_shift)
    image_gain, image_shift = wide(image_norm_gain), wide(image_norm_shift)

    bias_order = (
        text_cross_bias,
        image_cross_bias,
        text_inner_offset,
        image_inner_offset,
        text_self_bias,
        image_self_bias,
        text_outer_offset,
        image_outer_offset,
    )
    def spread(bias, blank):
        zero = jnp.zeros_like(bias[0])
        return [bias[0], zero, bias[1]] + ([zero] if blank else [])

    bias_row = jnp.concatenate(
        [
            *spread(text_cross_bias, False),
            *spread(image_cross_bias, False),
            text_inner_offset,
            image_inner_offset,
            *spread(text_self_bias, True),
            *spread(image_self_bias, False),
            text_outer_offset,
            image_outer_offset,
        ]
    ).reshape(1, -1)
    places = early_columns(
        3 * text_cross_bias.shape[1],
        3 * image_cross_bias.shape[1],
        text_inner_offset.shape[0],
        image_inner_offset.shape[0],
        4 * text_self_bias.shape[1],
        3 * image_self_bias.shape[1],
    )

    def turned(weight):
        return weight.reshape(weight.shape[0], -1).T

    def single(*locals_):
        return [(local, [local.shape[0]]) for local in locals_]

    text_qkv = turned(text_self_weight)
    text_both = jnp.concatenate([text_qkv, text_self_output], axis=0)
    stages = [
        single(turned(text_cross_weight), text_cross_output, turned(image_cross_weight), image_cross_output),
        single(turned(text_inner_expand), text_inner_reduce, turned(image_inner_expand), image_inner_reduce),
        [(text_both, [text_qkv.shape[0], text_self_output.shape[0]])]
        + single(turned(image_self_weight), image_self_output),
        single(turned(text_outer_expand), text_outer_reduce, turned(image_outer_expand), image_outer_reduce),
    ]

    cross_jobs = [
        (0, 1, CO_DH, text_cross_output.shape[0] // CO_DH, 0),
        (1, 0, CO_DH, image_cross_output.shape[0] // CO_DH, 0),
    ]
    self_jobs = [
        (0, 0, TS_DH, text_self_output.shape[0] // TS_DH, 3 * text_self_output.shape[0]),
        (1, 1, VS_DH, image_self_output.shape[0] // VS_DH, 0),
    ]

    def rows_of(bias, gain, shift):
        return [jnp.stack([wide(bias[k]), gain[k], shift[k]]) for k in range(4)]

    text_rows = rows_of(text_branch_bias, text_gain, text_shift)
    image_rows = rows_of(image_branch_bias, image_gain, image_shift)
    if dp == 8:
        early_rows = [item for pair in zip(text_rows[:3], image_rows[:3]) for item in pair]
        gathered, bias_rows, early = gather(
            stages, bias_row, (text, image), early_rows, ids, (cross_jobs, self_jobs), places
        )
    else:
        gathered, bias_rows = gather_plain(stages, bias_row)
    text_cw, text_co, image_cw, image_co = gathered[:4]
    text_ie, text_ir, image_ie, image_ir = gathered[4:8]
    text_sb, image_sw, image_so = gathered[8:11]
    text_oe, text_or, image_oe, image_or = gathered[11:]
    bias_rows = jnp.concatenate([bias_row, bias_rows.reshape(tensor - 1, -1)], axis=0)
    offsets = [bias_rows[:, at : at + size].reshape(1, -1) for at, size in places]

    if dp == 8:
        text_cross, image_cross, text_inner, image_inner, text_self, image_self = early
    else:
        text_cross, image_cross = mix_forward(
            "cross",
            cross_jobs,
            ids,
            [
                (text, text_cw, text_co, offsets[0], text_rows[0]),
                (image, image_cw, image_co, offsets[1], image_rows[0]),
            ],
        )
        text_inner, image_inner = ffn_forward(
            "inner",
            [
                (text_cross[2], text_ie, text_ir, offsets[2], text_rows[1]),
                (image_cross[2], image_ie, image_ir, offsets[3], image_rows[1]),
            ],
        )
        text_self, image_self = mix_forward(
            "self",
            self_jobs,
            ids,
            [
                (text_inner[2], text_sb, text_sb, offsets[4], text_rows[2]),
                (image_inner[2], image_sw, image_so, offsets[5], image_rows[2]),
            ],
        )
    text_outer, image_outer = ffn_forward(
        "outer",
        [
            (text_self[2], text_oe, text_or, offsets[6], text_rows[3]),
            (image_self[2], image_oe, image_or, offsets[7], image_rows[3]),
        ],
    )
    text_result, image_result = text_outer[2], image_outer[2]

    text_part, image_part = text.shape[1] // dp, image.shape[1] // dp
    text_hidden, image_hidden = text_inner_offset.shape[0], image_inner_offset.shape[0]

    def ffn_reduction(states, backs, kepts):
        chunks = []
        for k in range(2):
            chunks += plain_chunks(text_part, k, text_hidden)
        for k in range(2):
            chunks += plain_chunks(image_part, 2 + k, image_hidden)
        lefts = [item for k in range(2) for item in (states[k], backs[k][1])]
        rights = [item for k in range(2) for item in (backs[k][3], kepts[k][1])]
        return chunks, lefts, rights

    def mix_reduction(states, backs, kepts, chunks):
        lefts = [item for k in range(2) for item in (states[k], backs[k][1])]
        rights = [item for k in range(2) for item in (backs[k][3], kepts[k][1])]
        return chunks, lefts, rights

    if dp == 8:
        qkv = 3 * text_self_output.shape[0]
        ffn_groups = [
            (text_part, text_hidden // LANES, [(0, text_hidden, 0)]),
            (text_part, text_hidden // LANES, [(1, text_hidden, 0)]),
            (image_part, image_hidden // LANES, [(2, image_hidden, 0)]),
            (image_part, image_hidden // LANES, [(3, image_hidden, 0)]),
        ]
        text_cols, image_cols = text_cross_output.shape[0], image_cross_output.shape[0]
        cross_groups = [
            (text_part, 3 * text_cols // LANES, [(0, 3 * text_cols, 0)]),
            (text_part, text_cols // LANES, [(1, text_cols, 0)]),
            (image_part, 3 * image_cols // LANES, [(2, 3 * image_cols, 0)]),
            (image_part, image_cols // LANES, [(3, image_cols, 0)]),
        ]
        both, plain_part = text_both.shape[0], qkv // LANES
        image_cols = image_self_output.shape[0]
        self_groups = [
            (text_part, plain_part, [(0, both, 0)]),
            (text_part, 1, [(0, both, plain_part * LANES), (1, both, plain_part * LANES)]),
            (image_part, 3 * image_cols // LANES, [(2, 3 * image_cols, 0)]),
            (image_part, image_cols // LANES, [(3, image_cols, 0)]),
        ]
        all_stages = [
            ("ffn", None, ((11, 12), (13, 14)), 3, ffn_groups),
            ("mix", self_jobs, ((8, 8), (9, 10)), 2, self_groups),
            ("ffn", None, ((4, 5), (6, 7)), 1, ffn_groups),
            ("mix", cross_jobs, ((0, 1), (2, 3)), 0, cross_groups),
        ]
        counts = [
            sum(count * repeat for count, repeat, _ in stage[4]) for stage in all_stages
        ]
        values = [(text_outer, image_outer), (text_self, image_self)]
        values += [(text_inner, image_inner), (text_cross, image_cross)]
        inputs = [(text_self[2], image_self[2]), (text_inner[2], image_inner[2])]
        inputs += [(text_cross[2], image_cross[2]), (wide(text), wide(image))]
        saved = []
        for pair, states in zip(values, inputs):
            for (columns, active, _, normed, scale), state in zip(pair, states):
                saved += [columns, normed, scale, active, state]
        back_rows = []
        for norm in (3, 2, 1, 0):
            back_rows += [text_rows[norm], image_rows[norm]]
        packed, (delta_text, delta_image), bias_sum, shared_sums = backward_all(
            all_stages,
            counts,
            places,
            [item.reshape(tensor, -1, item.shape[1]) for item in gathered],
            saved,
            (wide(text_cotangent), wide(image_cotangent)),
            back_rows,
            ids,
        )
    else:
        outer_back = ffn_backward(
            "outer_back",
            [
                (wide(text_cotangent), text_outer, text_oe, text_or, text_rows[3]),
                (wide(image_cotangent), image_outer, image_oe, image_or, image_rows[3]),
            ],
        )
        outer = ffn_reduction((text_self[2], image_self[2]), outer_back, (text_outer, image_outer))
        upstream = (outer_back[0][0], outer_back[1][0])

        self_back = mix_backward(
            "self_back",
            self_jobs,
            ids,
            [
                (upstream[0], text_self, text_sb, text_sb, text_rows[2]),
                (upstream[1], image_self, image_sw, image_so, image_rows[2]),
            ],
        )
        mixed_width = 3 * text_self_output.shape[0]
        chunks = []
        for at in range(0, text_both.shape[0], LANES):
            terms = [(0, 0, at)] if at < mixed_width else []
            if at + LANES > mixed_width:
                terms.append((1, 1, at))
            chunks.append((text_part, terms))
        chunks += plain_chunks(image_part, 2, 3 * image_self_output.shape[0])
        chunks += plain_chunks(image_part, 3, image_self_output.shape[0])
        own = mix_reduction((text_inner[2], image_inner[2]), self_back, (text_self, image_self), chunks)
        upstream = (self_back[0][0], self_back[1][0])

        inner_back = ffn_backward(
            "inner_back",
            [
                (upstream[0], text_inner, text_ie, text_ir, text_rows[1]),
                (upstream[1], image_inner, image_ie, image_ir, image_rows[1]),
            ],
        )
        inner = ffn_reduction((text_cross[2], image_cross[2]), inner_back, (text_inner, image_inner))
        upstream = (inner_back[0][0], inner_back[1][0])

        cross_back = mix_backward(
            "cross_back",
            cross_jobs,
            ids,
            [
                (upstream[0], text_cross, text_cw, text_co, text_rows[0]),
                (upstream[1], image_cross, image_cw, image_co, image_rows[0]),
            ],
        )
        delta_text, delta_image = cross_back[0][0], cross_back[1][0]
        chunks = plain_chunks(text_part, 0, 3 * text_cross_output.shape[0])
        chunks += plain_chunks(text_part, 1, text_cross_output.shape[0])
        chunks += plain_chunks(image_part, 2, 3 * image_cross_output.shape[0])
        chunks += plain_chunks(image_part, 3, image_cross_output.shape[0])
        cross = mix_reduction((text, image), cross_back, (text_cross, image_cross), chunks)
        backs = (cross_back, inner_back, self_back, outer_back)
        bias_deltas = (
            bias_parts(cross_back[0][4], text_cross_output.shape[0]),
            bias_parts(cross_back[1][4], image_cross_output.shape[0]),
            inner_back[0][4],
            inner_back[1][4],
            bias_parts(self_back[0][4], text_self_output.shape[0]),
            bias_parts(self_back[1][4], image_self_output.shape[0]),
            outer_back[0][4],
            outer_back[1][4],
        )
        by_near = jnp.concatenate([item.reshape(tensor, -1) for item in bias_deltas], axis=1)
        by_place = jnp.stack(
            [lax.dynamic_index_in_dim(by_near, place_t ^ s, 0, False) for s in range(tensor)]
        )
        shared = tuple(
            jnp.stack([back[k][2][kind] for back in backs]) for k in range(2) for kind in range(3)
        )
        line = jnp.concatenate([by_place.reshape(-1)] + [item.reshape(-1) for item in shared])
        line = line.reshape(-1, 128)
        packed = [reduce_plain(*item) for item in (outer, own, inner, cross)]
        line = lax.psum(line, ("dp", "tensor")).reshape(-1)
    text_wide, image_wide = text_cross_output.shape[0], image_cross_output.shape[0]
    text_own, image_own = text_self_output.shape[0], image_self_output.shape[0]
    ffn_layout = [
        (text_part, text_hidden // LANES, [("flat", text_hidden)]),
        (text_part, text_hidden // LANES, [("turn", text_hidden)]),
        (image_part, image_hidden // LANES, [("flat", image_hidden)]),
        (image_part, image_hidden // LANES, [("turn", image_hidden)]),
    ]
    own_layout = [
        (text_part, 4 * text_own // LANES, [("cube", 3 * text_own), ("turn", text_own)]),
        (image_part, 3 * image_own // LANES, [("cube", 3 * image_own)]),
        (image_part, image_own // LANES, [("turn", image_own)]),
    ]
    cross_layout = [
        (text_part, 3 * text_wide // LANES, [("cube", 3 * text_wide)]),
        (text_part, text_wide // LANES, [("turn", text_wide)]),
        (image_part, 3 * image_wide // LANES, [("cube", 3 * image_wide)]),
        (image_part, image_wide // LANES, [("turn", image_wide)]),
    ]
    layouts = [ffn_layout, own_layout, ffn_layout, cross_layout]
    if dp == 8:
        smalls = [
            (at, item.shape[-1], item.ndim == 2) for item, (at, _) in zip(bias_order, places)
        ]
        deltas = unpack(packed, layouts, smalls, (bias_sum, *shared_sums))
    else:
        deltas = unpack(packed, layouts)
    text_oe_delta, text_or_delta, image_oe_delta, image_or_delta = deltas[:4]
    text_sw_delta, text_so_delta, image_sw_delta, image_so_delta = deltas[4:8]
    text_ie_delta, text_ir_delta, image_ie_delta, image_ir_delta = deltas[8:12]
    text_cw_delta, text_co_delta, image_cw_delta, image_co_delta = deltas[12:16]
    if dp == 8:
        bias_out = [value.reshape(item.shape) for value, item in zip(deltas[16:24], bias_order)]
        shared_out = deltas[24:]
    else:
        by_place = lax.dynamic_index_in_dim(
            line[: by_place.size].reshape(by_place.shape), place_t, 0, False
        )
        bias_out, at = [], 0
        for item in bias_order:
            size = math.prod(item.shape)
            bias_out.append(by_place[at : at + size].reshape(item.shape))
            at += size
        shared_out, at = [], math.prod(by_near.shape)
        for item in shared:
            shared_out.append(line[at : at + item.size].reshape(item.shape))
            at += item.size

    return (
        text_result,
        image_result,
        delta_text,
        delta_image,
        text_cw_delta,
        bias_out[0],
        text_co_delta,
        text_ie_delta,
        bias_out[2],
        text_ir_delta,
        text_sw_delta,
        bias_out[4],
        text_so_delta,
        text_oe_delta,
        bias_out[6],
        text_or_delta,
        shared_out[0],
        shared_out[1],
        shared_out[2],
        image_cw_delta,
        bias_out[1],
        image_co_delta,
        image_ie_delta,
        bias_out[3],
        image_ir_delta,
        image_sw_delta,
        bias_out[5],
        image_so_delta,
        image_oe_delta,
        bias_out[7],
        image_or_delta,
        shared_out[3],
        shared_out[4],
        shared_out[5],
    )


def solution(mesh):
    placed = (
        P(("dp", "tensor"), None),
        P(("dp", "tensor"), None),
        P("dp", None),
        P("dp", None),
        P(None, None, "tensor"),
        P(None, "tensor"),
        P("tensor", None),
        P(None, "tensor"),
        P("tensor"),
        P("tensor", None),
        P(None, None, "tensor"),
        P(None, "tensor"),
        P("tensor", None),
        P(None, "tensor"),
        P("tensor"),
        P("tensor", None),
        P(),
        P(),
        P(),
        P(None, None, "tensor"),
        P(None, "tensor"),
        P("tensor", None),
        P(None, "tensor"),
        P("tensor"),
        P("tensor", None),
        P(None, None, "tensor"),
        P(None, "tensor"),
        P("tensor", None),
        P(None, "tensor"),
        P("tensor"),
        P("tensor", None),
        P(),
        P(),
        P(),
        P(("dp", "tensor"), None),
        P(("dp", "tensor"), None),
    )
    return jax.shard_map(
        per_device,
        mesh=mesh,
        in_specs=placed,
        out_specs=(
            P(("dp", "tensor"), None),
            P(("dp", "tensor"), None),
            P(("dp", "tensor"), None),
            P(("dp", "tensor"), None),
            P("dp", None, "tensor"),
            P(None, "tensor"),
            P("tensor", "dp"),
            P("dp", "tensor"),
            P("tensor"),
            P("tensor", "dp"),
            P("dp", None, "tensor"),
            P(None, "tensor"),
            P("tensor", "dp"),
            P("dp", "tensor"),
            P("tensor"),
            P("tensor", "dp"),
            P(),
            P(),
            P(),
            P("dp", None, "tensor"),
            P(None, "tensor"),
            P("tensor", "dp"),
            P("dp", "tensor"),
            P("tensor"),
            P("tensor", "dp"),
            P("dp", None, "tensor"),
            P(None, "tensor"),
            P("tensor", "dp"),
            P("dp", "tensor"),
            P("tensor"),
            P("tensor", "dp"),
            P(),
            P(),
            P(),
        ),
        check_vma=False,
    )
```
